256 devices in a mesh: ctx: 16 (over x, z_hi, core), head: 16 (over z_lo, y).
Axes of the slice: x: 4, y: 4, z: 8 (z_hi: 2, z_lo: 4; z = z_hi * 4 + z_lo), core: 2. Of those that a mesh axis runs over, the one named last changes fastest.
Arguments:
- queries: bfloat16 [36864, 2048], P(('ctx', 'head')), may hold values from -8 to 8
- keys: bfloat16 [36864, 2048], P(('ctx', 'head')), may hold values from -8 to 8
- values: bfloat16 [36864, 2048], P(('ctx', 'head')), may hold values from -6 to 6
- out_grad: bfloat16 [36864, 2048], P(('ctx', 'head')), may hold values from -6 to 6
- key_tiles: int32 [16, 192, 9], P('head', 'ctx'), may hold values from -1 to 191, as said below
Outputs:
- attention_out: bfloat16 [36864, 2048], P(('ctx', 'head'))
- query_grad: bfloat16 [36864, 2048], P(('ctx', 'head'))
- key_grad: bfloat16 [36864, 2048], P(('ctx', 'head'))
- value_grad: bfloat16 [36864, 2048], P(('ctx', 'head'))
The draws below stay inside these ranges and needn't reach their ends.
Inputs may be any that keep to these rules, and one draw needn't show every extreme that they name: `key_tiles`: row (h, i) lists in ascending order, then -1 to fill 9 places, the tiles of a grid of 8 time slabs of 3 by 8 tiles (tile i in slab i // 24, tile row (i % 24) // 8, tile column i % 8) that differ from tile i by at most one along tile columns and along one more direction fixed for each head, time or tile rows, and not at all along the third. Both kinds of head occur, and some rows are full.
All inputs are finite; a program needn't handle non-finite values.
Results may differ from the reference program's by a relative error of at most 0.02.
Values may be sent and summed in bfloat16 or wider, within the bound.
A program may use at most 128 MiB of HBM per device.

```python
import math
import jax
import jax.numpy as jnp
from jax import lax

DH = 128
TILE = 192
GROUP_TILES = 12
GH = 3
GW = 8
SLAB = 24
KMAX = 9
HEADS = 16
HD = 2048
NT = 192
TOKENS = 36864
N_CTX = 16


def paired_fields(key):
    query_field = jnp.clip(jax.random.normal(jax.random.fold_in(key, 11), (TOKENS, HD), jnp.float32), -4.0, 4.0)
    key_field = jnp.clip(jax.random.normal(jax.random.fold_in(key, 12), (TOKENS, HD), jnp.float32), -4.0, 4.0)
    return (query_field, key_field)


def draw_queries(key, part):
    return paired_fields(key)[0].astype(jnp.bfloat16)


def draw_keys(key, part):
    return paired_fields(key)[1].astype(jnp.bfloat16)


def draw_key_tiles(key, part):
    kinds = jax.random.permutation(jax.random.fold_in(key, 31), HEADS) % 2
    tiles = jnp.arange(NT, dtype=jnp.int32)
    frame = tiles // SLAB
    tile_row = tiles % SLAB // GW
    column = tiles % GW
    outer = jnp.array([-1, -1, -1, 0, 0, 0, 1, 1, 1], jnp.int32)
    inner = jnp.array([-1, 0, 1, -1, 0, 1, -1, 0, 1], jnp.int32)
    step_time = jnp.where(kinds[:, None] == 0, outer[None, :], 0)
    step_row = jnp.where(kinds[:, None] == 1, outer[None, :], 0)
    new_frame = frame[None, :, None] + step_time[:, None, :]
    new_row = tile_row[None, :, None] + step_row[:, None, :]
    new_column = column[None, :, None] + inner[None, None, :] + 0 * new_frame
    inside = (new_frame >= 0) & (new_frame < NT // SLAB) & (new_row >= 0) & (new_row < GH) & (new_column >= 0) & (new_column < GW)
    index = new_frame * SLAB + new_row * GW + new_column
    ranked = jnp.sort(jnp.where(inside, index, NT), axis=-1)[:, :, :KMAX]
    return jnp.where(ranked >= NT, -1, ranked).astype(jnp.int32)


def shard_levels(key, shape, cuts, least, top_value):
    def one(dim, blocks):
        draws = jax.random.uniform(jax.random.fold_in(jax.random.fold_in(key, 6), dim), (blocks,), jnp.float32, least / len(cuts), top_value / len(cuts))
        return jnp.repeat(jnp.exp(draws), shape[dim] // blocks).reshape((-1,) + (1,) * (len(shape) - dim - 1))

    gain = one(*cuts[0])
    for cut in cuts[1:]:
        gain = gain * one(*cut)
    return gain


def gaussian(own_key, dims, scale, limit, cuts=(), held_as=jnp.bfloat16):
    gain = shard_levels(own_key, dims, cuts, -0.22, 0.18) if cuts else 1.0
    drawn = jax.random.normal(own_key, dims, jnp.float32) * scale * gain
    return jnp.minimum(jnp.maximum(drawn, -limit), limit).astype(held_as)


def setup_inputs(seed: int = 0) -> dict:
    key_of = jax.random.split(jax.random.key(seed), 6)
    return {
        "queries": draw_queries(jax.random.fold_in(key_of[5], 71), 0),
        "keys": draw_keys(jax.random.fold_in(key_of[5], 71), 0),
        "values": gaussian(key_of[2], (TOKENS, HD), 1.0, 6.0, ((0, 256),)),
        "out_grad": gaussian(key_of[3], (TOKENS, HD), 1.0, 6.0, ((0, 256),)),
        "key_tiles": draw_key_tiles(jax.random.fold_in(key_of[5], 71), 0),
    }


NEG_FILL = -1e+30

def tile_block(query_rows, grad_rows, key_rows, value_rows, present, score_scale):
    query_wide = query_rows.astype(jnp.float32)
    key_wide = key_rows.astype(jnp.float32)
    value_wide = value_rows.astype(jnp.float32)
    grad_wide = grad_rows.astype(jnp.float32)
    scores = jnp.einsum('aqd,akjd->aqkj', query_wide, key_wide) * score_scale
    scores = jnp.where(present[:, None, :, None], scores, NEG_FILL)
    row_top = lax.optimization_barrier(jnp.max(scores, axis=(2, 3), keepdims=True))
    raised = jnp.exp(scores - row_top)
    probs = raised / lax.optimization_barrier(jnp.sum(raised, axis=(2, 3), keepdims=True))
    weights = lax.optimization_barrier(probs.astype(jnp.bfloat16)).astype(jnp.float32)
    attended = lax.optimization_barrier(jnp.einsum('aqkj,akjd->aqd', weights, value_wide).astype(jnp.bfloat16))
    row_delta = lax.optimization_barrier(jnp.sum(grad_wide * attended.astype(jnp.float32), axis=2))[:, :, None, None]
    weight_grad = jnp.einsum('aqd,akjd->aqkj', grad_wide, value_wide)
    score_grad = lax.optimization_barrier((weights * (weight_grad - row_delta) * score_scale).astype(jnp.bfloat16)).astype(jnp.float32)
    query_grad = jnp.einsum('aqkj,akjd->aqd', score_grad, key_wide).astype(jnp.bfloat16)
    key_part = jnp.einsum('aqkj,aqd->akjd', score_grad, query_wide)
    value_part = jnp.einsum('aqkj,aqd->akjd', weights, grad_wide)
    return (attended, query_grad, key_part, value_part)

def reference(queries, keys, values, out_grad, key_tiles):
    score_scale = 1.0 / math.sqrt(DH)

    def head_pass(head_index):
        start_col = (head_index * DH).astype(jnp.int32)

        def head_slice(matrix):
            return lax.dynamic_slice_in_dim(matrix, start_col, DH, 1).reshape(NT, TILE, DH)
        query_tiles = head_slice(queries)
        key_all = head_slice(keys)
        value_all = head_slice(values)
        grad_tiles = head_slice(out_grad)
        tile_lists = lax.dynamic_index_in_dim(key_tiles, head_index, 0, keepdims=False)

        def group_pass(totals, group_index):
            first_tile = (group_index * GROUP_TILES).astype(jnp.int32)
            query_rows = lax.dynamic_slice_in_dim(query_tiles, first_tile, GROUP_TILES, 0)
            grad_rows = lax.dynamic_slice_in_dim(grad_tiles, first_tile, GROUP_TILES, 0)
            picked = lax.dynamic_slice_in_dim(tile_lists, first_tile, GROUP_TILES, 0)
            present = picked >= 0
            safe_tiles = jnp.where(present, picked, 0).astype(jnp.int32)
            attended, query_grad, key_part, value_part = tile_block(query_rows, grad_rows, key_all[safe_tiles], value_all[safe_tiles], present, score_scale)
            flat_tiles = safe_tiles.reshape(-1)
            key_sum = jnp.zeros((NT, TILE, DH), jnp.float32).at[flat_tiles].add(key_part.reshape(-1, TILE, DH))
            value_sum = jnp.zeros((NT, TILE, DH), jnp.float32).at[flat_tiles].add(value_part.reshape(-1, TILE, DH))
            key_round = lax.optimization_barrier(key_sum.astype(jnp.bfloat16)).astype(jnp.float32)
            value_round = lax.optimization_barrier(value_sum.astype(jnp.bfloat16)).astype(jnp.float32)
            return ((totals[0] + key_round, totals[1] + value_round), (attended, query_grad))
        zero_sum = jnp.zeros((NT, TILE, DH), jnp.float32)
        sums, produced = lax.scan(group_pass, (zero_sum, zero_sum), jnp.arange(N_CTX, dtype=jnp.int32))
        return (produced[0].reshape(TOKENS, DH), produced[1].reshape(TOKENS, DH), sums[0].astype(jnp.bfloat16).reshape(TOKENS, DH), sums[1].astype(jnp.bfloat16).reshape(TOKENS, DH))
    results = lax.map(head_pass, jnp.arange(HEADS, dtype=jnp.int32))

    def spread(matrix):
        return jnp.transpose(matrix, (1, 0, 2)).reshape(TOKENS, HEADS * DH)
    return (spread(results[0]), spread(results[1]), spread(results[2]), spread(results[3]))
```

```python
import math

import jax
import jax.numpy as jnp
from jax import lax
from jax.experimental import pallas as pl
from jax.experimental.pallas import tpu as pltpu
from jax.sharding import PartitionSpec as P

DH = 128
TILE = 192
HEADS = 16
PART = 48
ROWS = 144
COLS = 2 * TILE
SPAN = 4 * TILE
REACHED = 3 * TILE
NEG_FILL = -1e30
SCALE = 1.0 / math.sqrt(DH)
MESH = pl.DeviceIdType.MESH
VMEM_LIMIT = 60 * 1024 * 1024


def div(a, b):
    return lax.div(a, jnp.int32(b))


def rem(a, b):
    return lax.rem(a, jnp.int32(b))


def spot():
    ctx, sub = lax.axis_index("ctx"), lax.axis_index("head")
    core, z_hi, x = rem(ctx, 2), rem(div(ctx, 2), 2), div(ctx, 4)
    y, z_lo = rem(sub, 4), div(sub, 4)
    z = z_hi * 4 + z_lo
    head = 2 * z + div(y, 2)
    quarter = 2 * rem(y, 2) + core
    return dict(x=x, y=y, z=z, z_hi=z_hi, sub=sub, core=core, head=head, quarter=quarter)


def worker(x, head, quarter):
    z = div(head, 2)
    y = 2 * rem(head, 2) + div(quarter, 2)
    return (x * 4 + div(z, 4) * 2 + rem(quarter, 2), rem(z, 4) * 4 + y)


def copy_to(src, dst, send, recv, device):
    return pltpu.make_async_remote_copy(
        src_ref=src, dst_ref=dst, send_sem=send, recv_sem=recv, device_id=device, device_id_type=MESH
    )


def wait_bytes(ref, sem):
    pltpu.make_async_copy(ref, ref, sem).wait()


def gather_kernel(
    keys, values, queries, grads, flags, kv, qg, kinds, send_kv, recv_kv, send_qg, recv_qg, send_n, recv_n, kind_sems
):
    me = spot()
    x, z_hi, core, head, quarter = me["x"], me["z_hi"], me["core"], me["head"], me["quarter"]

    def part_place(k):
        at = me["sub"] * 3 + k
        tile = core * 12 + div(at, 4)
        column = rem(tile, 8)
        return div(tile, 8), div(column, 2), rem(column, 2), rem(at, 4)

    def send_head(target_head, own_head):
        for pair, out, send, recv, slab, shift in (
            ((keys, values), kv, send_kv, recv_kv, 1 + z_hi, 1),
            ((queries, grads), qg, send_qg, recv_qg, z_hi, 0),
        ):
            for k in range(3):
                row, to, side, part = part_place(k)
                first = pl.multiple_of((side + shift) * TILE + part * PART, 16)
                for a in range(2):
                    src = pair[a].at[pl.ds(k * PART, PART), pl.ds(pl.multiple_of(target_head * DH, DH), DH)]
                    dst = out.at[a, slab, row, pl.ds(first, PART), :]
                    if own_head:

                        @pl.when(to == quarter)
                        def _():
                            pltpu.make_async_copy(src, dst, recv).start()

                        @pl.when(to != quarter)
                        def _():
                            copy_to(src, dst, send, recv, worker(x, target_head, to)).start()

                    else:
                        copy_to(src, dst, send, recv, worker(x, target_head, to)).start()

    asker = (
        x * 4 + div(me["sub"], 8) * 2 + core,
        rem(div(me["sub"], 2), 4) * 4 + 2 * rem(me["sub"], 2) + z_hi,
    )
    own_kind = me["sub"] == head
    own_kind = jnp.logical_and(own_kind, rem(me["y"], 2) == z_hi)

    @pl.when(own_kind)
    def _():
        pltpu.make_async_copy(flags, kinds, kind_sems.at[1]).start()

    @pl.when(jnp.logical_not(own_kind))
    def _():
        copy_to(flags, kinds, kind_sems.at[0], kind_sems.at[1], asker).start()

    @pl.loop(1, HEADS)
    def _(step):
        send_head(rem(head + step, HEADS), False)

    send_head(head, True)

    own = kv.at[:, 1:3, :, TILE : TILE + COLS, :]
    wait_bytes(own, recv_kv)

    after = worker(rem(x + 1, 4), head, quarter)
    before = worker(rem(x + 3, 4), head, quarter)
    right = worker(x, head, rem(quarter + 1, 4))
    left = worker(x, head, rem(quarter + 3, 4))
    mine = slice(TILE, TILE + COLS)

    def halo(n, src, dst, device):
        return copy_to(src, dst, send_n.at[n], recv_n.at[n], device)

    forward = halo(0, kv.at[:, 2, :, mine, :], kv.at[:, 0, :, mine, :], after)
    backward = halo(1, kv.at[:, 1, :, mine, :], kv.at[:, 3, :, mine, :], before)
    forward.start()
    backward.start()
    hi, lo = slice(2 * TILE, 3 * TILE), slice(TILE, 2 * TILE)
    top, bottom = slice(3 * TILE, 4 * TILE), slice(0, TILE)
    inner = (
        halo(2, kv.at[:, 1:3, :, hi, :], kv.at[:, 1:3, :, bottom, :], right),
        halo(3, kv.at[:, 1:3, :, lo, :], kv.at[:, 1:3, :, top, :], left),
    )
    for c in inner:
        c.start()
    outer = []
    for n, slab, first in ((4, 0, forward), (6, 3, backward)):
        first.wait_recv()
        pair = (
            halo(n, kv.at[:, slab, :, hi, :], kv.at[:, slab, :, bottom, :], right),
            halo(n + 1, kv.at[:, slab, :, lo, :], kv.at[:, slab, :, top, :], left),
        )
        for c in pair:
            c.start()
        outer.extend(pair)
    for c in inner:
        c.wait()
    for c in outer:
        c.wait()
    forward.wait_send()
    backward.wait_send()
    wait_bytes(qg, recv_qg)
    own_parts = sum(
        (part_place(k)[1] == quarter).astype(jnp.int32) for k in range(3)
    )
    for count in range(4):

        @pl.when(own_parts == count)
        def _():
            sent = kv.at[:, 0, :, 0 : SPAN - 16 * count, :]
            wait_bytes(sent, send_kv)
            wait_bytes(sent, send_qg)

    wait_bytes(kinds, kind_sems.at[1])

    @pl.when(jnp.logical_not(own_kind))
    def _():
        wait_bytes(flags, kind_sems.at[0])


def work_kernel(kinds, kv, qg, outs, dkv, acc):
    me = spot()
    along_time = kinds[0, 0] > 0
    step_t = jnp.where(along_time, 1, 0)
    acc[...] = jnp.zeros_like(acc)

    def one_tile(t, masked, slab, row, side):
        first = pl.multiple_of(side * TILE, 64)
        q = qg[0, slab, row, pl.ds(first, TILE), :]
        g = qg[1, slab, row, pl.ds(first, TILE), :]
        span = pl.ds(first, REACHED)
        where = []
        scores = []
        for n in range(3):
            s_at = jnp.where(along_time, slab + n, slab + 1)
            r_at = jnp.where(along_time, row, jnp.clip(row + n - 1, 0, 2))
            where.append((s_at, r_at))
            k_rows = kv[0, s_at, r_at, span, :]
            s = lax.dot_general(q, k_rows, (((1,), (1,)), ((), ())), preferred_element_type=jnp.float32)
            if masked:
                ok_time = jnp.logical_and(2 * me["x"] + slab + n - 1 >= 0, 2 * me["x"] + slab + n - 1 < 8)
                ok_row = jnp.logical_and(row + n - 1 >= 0, row + n - 1 < 3)
                ok = jnp.where(along_time, ok_time.astype(jnp.int32), ok_row.astype(jnp.int32))
                column = 2 * me["quarter"] + side
                low = jnp.where(column > 0, 0, TILE)
                high = jnp.where(column < 7, REACHED, 2 * TILE) * ok
                lane = lax.broadcasted_iota(jnp.int32, s.shape, 1)
                s = jnp.where(jnp.logical_and(lane >= low, lane < high), s, NEG_FILL)
            scores.append(s)
        top = jnp.max(jnp.maximum(jnp.maximum(scores[0], scores[1]), scores[2]), axis=1, keepdims=True)
        raised = [jnp.exp((s - top) * SCALE) for s in scores]
        total = jnp.sum(raised[0] + raised[1] + raised[2], axis=1, keepdims=True)
        share = 1.0 / total
        weights = [(r * share).astype(jnp.bfloat16) for r in raised]
        attended = jnp.zeros((TILE, DH), jnp.float32)
        for n in range(3):
            v_rows = kv[1, where[n][0], where[n][1], span, :]
            attended += jnp.dot(weights[n], v_rows, preferred_element_type=jnp.float32)
        attended = attended.astype(jnp.bfloat16)
        outs[0, slab, row, pl.ds(first, TILE), :] = attended
        delta = jnp.sum(g.astype(jnp.float32) * attended.astype(jnp.float32), axis=1, keepdims=True)
        q_grad = jnp.zeros((TILE, DH), jnp.float32)
        for n in range(3):
            s_at, r_at = where[n]
            v_rows = kv[1, s_at, r_at, span, :]
            w_grad = lax.dot_general(g, v_rows, (((1,), (1,)), ((), ())), preferred_element_type=jnp.float32)
            s_grad = (weights[n].astype(jnp.float32) * (w_grad - delta) * SCALE).astype(jnp.bfloat16)
            k_rows = kv[0, s_at, r_at, span, :]
            q_grad += jnp.dot(s_grad, k_rows, preferred_element_type=jnp.float32)
            acc[0, s_at, r_at, span, :] += lax.dot_general(
                s_grad, q, (((0,), (0,)), ((), ())), preferred_element_type=jnp.float32
            )
            acc[1, s_at, r_at, span, :] += lax.dot_general(
                weights[n], g, (((0,), (0,)), ((), ())), preferred_element_type=jnp.float32
            )
        outs[1, slab, row, pl.ds(first, TILE), :] = q_grad.astype(jnp.bfloat16)

    @pl.loop(0, 12)
    def _(t):
        slab, row, side = div(t, 6), rem(div(t, 2), 3), rem(t, 2)
        column = 2 * me["quarter"] + side
        slab_at = 2 * me["x"] + slab
        inside = jnp.where(
            along_time,
            jnp.logical_and(slab_at > 0, slab_at < 7).astype(jnp.int32),
            (row == 1).astype(jnp.int32),
        )
        full = jnp.logical_and(inside == 1, jnp.logical_and(column > 0, column < 7))

        @pl.when(full)
        def _():
            one_tile(t, False, slab, row, side)

        @pl.when(jnp.logical_not(full))
        def _():
            one_tile(t, True, slab, row, side)

    for s_at in range(4):
        for r_at in range(3):
            for a in range(2):
                dkv[a, s_at, r_at] = acc[a, s_at, r_at].astype(jnp.bfloat16)


def scatter_kernel(
    outs, dkv, attended, q_grad, k_grad, v_grad, from_side, from_slab, summed, final,
    send_o, recv_o, send_d, recv_d, send_n, recv_n
):
    me = spot()
    x, head, quarter = me["x"], me["head"], me["quarter"]

    def send_parts(src_of, targets, send, recv):
        @pl.loop(0, 48)
        def _(step):
            n = rem(step + 3 * head, 48)
            slab, row, side, part = div(n, 24), div(rem(n, 24), 8), rem(div(n, 4), 2), rem(n, 4)
            tile = row * 8 + 2 * quarter + side
            at = rem(tile, 12) * 4 + part
            core, sub, k = div(tile, 12), div(at, 3), rem(at, 3)
            ctx = x * 4 + slab * 2 + core
            self_part = jnp.logical_and(ctx == lax.axis_index("ctx"), sub == me["sub"])
            first = pl.multiple_of(side * TILE + part * PART, 16)
            for a in range(2):
                src = src_of(a, slab, row, pl.ds(first, PART))
                dst = targets[a].at[
                    pl.ds(pl.multiple_of(k * PART, 16), PART), pl.ds(pl.multiple_of(head * DH, DH), DH)
                ]

                @pl.when(self_part)
                def _():
                    pltpu.make_async_copy(src, dst, recv).start()

                @pl.when(jnp.logical_not(self_part))
                def _():
                    copy_to(src, dst, send, recv, (ctx, sub)).start()

    send_parts(lambda a, s, r, rows: outs.at[a, s, r, rows, :], (attended, q_grad), send_o, recv_o.at[0])

    right = worker(x, head, rem(quarter + 1, 4))
    left = worker(x, head, rem(quarter + 3, 4))
    to_left = copy_to(dkv.at[:, :, :, 0:TILE, :], from_side.at[1], send_n.at[1], recv_n.at[1], left)
    to_right = copy_to(
        dkv.at[:, :, :, 3 * TILE : 4 * TILE, :], from_side.at[0], send_n.at[0], recv_n.at[0], right
    )
    @pl.when(quarter > 0)
    def _():
        to_left.start()

    @pl.when(quarter < 3)
    def _():
        to_right.start()

    for side in range(2):
        has = quarter > 0 if side == 0 else quarter < 3
        here = slice((1 + side) * TILE, (2 + side) * TILE)
        there = slice(side * TILE, (1 + side) * TILE)

        @pl.when(has)
        def _():
            wait_bytes(from_side.at[side], recv_n.at[side])
            for a in range(2):
                for s in range(4):
                    summed[a, s, :, there, :] = (
                        dkv[a, s, :, here, :].astype(jnp.float32) + from_side[side, a, s].astype(jnp.float32)
                    ).astype(jnp.bfloat16)

        @pl.when(jnp.logical_not(has))
        def _():
            for a in range(2):
                for s in range(4):
                    summed[a, s, :, there, :] = dkv[a, s, :, here, :]

    after = worker(rem(x + 1, 4), head, quarter)
    before = worker(rem(x + 3, 4), head, quarter)
    to_after = copy_to(summed.at[:, 3], from_slab.at[0], send_n.at[2], recv_n.at[2], after)
    to_before = copy_to(summed.at[:, 0], from_slab.at[1], send_n.at[3], recv_n.at[3], before)

    @pl.when(x < 3)
    def _():
        to_after.start()

    @pl.when(x > 0)
    def _():
        to_before.start()

    for slab in range(2):
        has = x > 0 if slab == 0 else x < 3

        @pl.when(has)
        def _():
            wait_bytes(from_slab.at[slab], recv_n.at[2 + slab])
            for a in range(2):
                final[a, slab] = (
                    summed[a, 1 + slab].astype(jnp.float32) + from_slab[slab, a].astype(jnp.float32)
                ).astype(jnp.bfloat16)

        @pl.when(jnp.logical_not(has))
        def _():
            for a in range(2):
                final[a, slab] = summed[a, 1 + slab]

    send_parts(lambda a, s, r, rows: final.at[a, s, r, rows, :], (k_grad, v_grad), send_d, recv_d.at[0])

    @pl.when(quarter > 0)
    def _():
        to_left.wait_send()

    @pl.when(quarter < 3)
    def _():
        to_right.wait_send()

    @pl.when(x < 3)
    def _():
        to_after.wait_send()

    @pl.when(x > 0)
    def _():
        to_before.wait_send()

    def own_part(k):
        at = me["sub"] * 3 + k
        tile = me["core"] * 12 + div(at, 4)
        return (div(rem(tile, 8), 2) == quarter).astype(jnp.int32)

    own_parts = own_part(0) + own_part(1) + own_part(2)
    for count in range(4):

        @pl.when(own_parts == count)
        def _():
            sent = dkv.at[:, 0, :, 0 : SPAN - 16 * count, :]
            wait_bytes(sent, send_o)
            wait_bytes(sent, send_d)

    wait_bytes(outs, recv_o.at[0])
    wait_bytes(final, recv_d.at[0])


def per_device(queries, keys, values, out_grad, key_tiles):
    ctx = lax.axis_index("ctx")
    own_slab = ctx // 2
    lists = key_tiles[0]
    along_time = jnp.any(jnp.logical_and(lists >= 0, lists // 24 != own_slab))
    flags = jnp.broadcast_to(along_time.astype(jnp.int32), (8, 128))

    anywhere = pl.BlockSpec(memory_space=pl.ANY)
    vmem = pl.BlockSpec(memory_space=pltpu.VMEM)
    kv, qg, kinds = pl.pallas_call(
        gather_kernel,
        name="gather_heads",
        out_shape=(
            jax.ShapeDtypeStruct((2, 4, 3, SPAN, DH), jnp.bfloat16),
            jax.ShapeDtypeStruct((2, 2, 3, COLS, DH), jnp.bfloat16),
            jax.ShapeDtypeStruct((8, 128), jnp.int32),
        ),
        in_specs=[anywhere] * 5,
        out_specs=(anywhere, anywhere, anywhere),
        scratch_shapes=[
            pltpu.SemaphoreType.DMA,
            pltpu.SemaphoreType.DMA,
            pltpu.SemaphoreType.DMA,
            pltpu.SemaphoreType.DMA,
            pltpu.SemaphoreType.DMA((8,)),
            pltpu.SemaphoreType.DMA((8,)),
            pltpu.SemaphoreType.DMA((2,)),
        ],
        compiler_params=pltpu.CompilerParams(has_side_effects=True),
    )(keys, values, queries, out_grad, flags)

    outs, dkv = pl.pallas_call(
        work_kernel,
        name="tile_attention",
        out_shape=(
            jax.ShapeDtypeStruct((2, 2, 3, COLS, DH), jnp.bfloat16),
            jax.ShapeDtypeStruct((2, 4, 3, SPAN, DH), jnp.bfloat16),
        ),
        in_specs=[pl.BlockSpec(memory_space=pltpu.SMEM), vmem, vmem],
        out_specs=(vmem, vmem),
        scratch_shapes=[pltpu.VMEM((2, 4, 3, SPAN, DH), jnp.float32)],
        compiler_params=pltpu.CompilerParams(vmem_limit_bytes=VMEM_LIMIT),
    )(kinds, kv, qg)

    token_block = jax.ShapeDtypeStruct((ROWS, HEADS * DH), jnp.bfloat16)
    return pl.pallas_call(
        scatter_kernel,
        name="scatter_heads",
        out_shape=(token_block,) * 4,
        in_specs=[anywhere, vmem],
        out_specs=(anywhere,) * 4,
        scratch_shapes=[
            pltpu.VMEM((2, 2, 4, 3, TILE, DH), jnp.bfloat16),
            pltpu.VMEM((2, 2, 3, COLS, DH), jnp.bfloat16),
            pltpu.VMEM((2, 4, 3, COLS, DH), jnp.bfloat16),
            pltpu.VMEM((2, 2, 3, COLS, DH), jnp.bfloat16),
            pltpu.SemaphoreType.DMA,
            pltpu.SemaphoreType.DMA((1,)),
            pltpu.SemaphoreType.DMA,
            pltpu.SemaphoreType.DMA((1,)),
            pltpu.SemaphoreType.DMA((4,)),
            pltpu.SemaphoreType.DMA((4,)),
        ],
        compiler_params=pltpu.CompilerParams(has_side_effects=True, vmem_limit_bytes=VMEM_LIMIT),
    )(outs, dkv)


def solution(mesh):
    token_spec = P(("ctx", "head"), None)
    return jax.shard_map(
        per_device,
        mesh=mesh,
        in_specs=(token_spec,) * 4 + (P("head", "ctx", None),),
        out_specs=(token_spec,) * 4,
        check_vma=False,
    )
```

```python
import math

import jax
import jax.numpy as jnp
from jax import lax
from jax.experimental import pallas as pl
from jax.experimental.pallas import tpu as pltpu
from jax.sharding import PartitionSpec as P

DH = 128
TILE = 192
HEADS = 16
PART = 48
ROWS = 144
COLS = 2 * TILE
SPAN = 4 * TILE
REACHED = 3 * TILE
NEG_FILL = -1e30
SCALE = 1.0 / math.sqrt(DH)
MESH = pl.DeviceIdType.MESH
VMEM_LIMIT = 60 * 1024 * 1024


def div(a, b):
    return lax.div(a, jnp.int32(b))


def rem(a, b):
    return lax.rem(a, jnp.int32(b))


def spot():
    ctx, sub = lax.axis_index("ctx"), lax.axis_index("head")
    core, z_hi, x = rem(ctx, 2), rem(div(ctx, 2), 2), div(ctx, 4)
    y, z_lo = rem(sub, 4), div(sub, 4)
    z = z_hi * 4 + z_lo
    head = 2 * z + div(y, 2)
    quarter = 2 * rem(y, 2) + core
    return dict(x=x, y=y, z=z, z_hi=z_hi, sub=sub, core=core, head=head, quarter=quarter)


def worker(x, head, quarter):
    z = div(head, 2)
    y = 2 * rem(head, 2) + div(quarter, 2)
    return (x * 4 + div(z, 4) * 2 + rem(quarter, 2), rem(z, 4) * 4 + y)


def copy_to(src, dst, send, recv, device):
    return pltpu.make_async_remote_copy(
        src_ref=src, dst_ref=dst, send_sem=send, recv_sem=recv, device_id=device, device_id_type=MESH
    )


def greet(me):
    barrier = pltpu.get_barrier_semaphore()
    x = me["x"]
    own = me["sub"] * 4 + me["z_hi"] * 2 + me["core"]

    @pl.loop(1, 64)
    def _(step):
        other = rem(own + step, 64)
        device = (x * 4 + rem(other, 4), div(other, 4))
        pl.semaphore_signal(barrier, inc=1, device_id=device, device_id_type=MESH)

    here = me["z_hi"] * 2 + me["core"]
    for step in (1, 3):
        device = (rem(x + step, 4) * 4 + here, me["sub"])
        pl.semaphore_signal(barrier, inc=1, device_id=device, device_id_type=MESH)
    pl.semaphore_wait(barrier, 65)


def wait_bytes(ref, sem):
    pltpu.make_async_copy(ref, ref, sem).wait()


def gather_kernel(
    keys, values, queries, grads, flags, kv, qg, kinds, send_kv, recv_kv, send_qg, recv_qg, send_n, recv_n, kind_sems
):
    me = spot()
    x, z_hi, core, head, quarter = me["x"], me["z_hi"], me["core"], me["head"], me["quarter"]

    def part_place(k):
        at = me["sub"] * 3 + k
        tile = core * 12 + div(at, 4)
        column = rem(tile, 8)
        return div(tile, 8), div(column, 2), rem(column, 2), rem(at, 4)

    greet(me)

    def send_head(which, target_head, own_head):
        for pair, out, send, recv, slab, shift in (which,):
            for k in range(3):
                row, to, side, part = part_place(k)
                first = pl.multiple_of((side + shift) * TILE + part * PART, 16)
                for a in range(2):
                    src = pair[a].at[pl.ds(k * PART, PART), pl.ds(pl.multiple_of(target_head * DH, DH), DH)]
                    dst = out.at[a, slab, row, pl.ds(first, PART), :]
                    if own_head:

                        @pl.when(to == quarter)
                        def _():
                            pltpu.make_async_copy(src, dst, recv).start()

                        @pl.when(to != quarter)
                        def _():
                            copy_to(src, dst, send, recv, worker(x, target_head, to)).start()

                    else:
                        copy_to(src, dst, send, recv, worker(x, target_head, to)).start()

    asker = (
        x * 4 + div(me["sub"], 8) * 2 + core,
        rem(div(me["sub"], 2), 4) * 4 + 2 * rem(me["sub"], 2) + z_hi,
    )
    own_kind = me["sub"] == head
    own_kind = jnp.logical_and(own_kind, rem(me["y"], 2) == z_hi)

    @pl.when(own_kind)
    def _():
        pltpu.make_async_copy(flags, kinds, kind_sems.at[1]).start()

    @pl.when(jnp.logical_not(own_kind))
    def _():
        copy_to(flags, kinds, kind_sems.at[0], kind_sems.at[1], asker).start()

    for which in (
        ((keys, values), kv, send_kv, recv_kv, 1 + z_hi, 1),
        ((queries, grads), qg, send_qg, recv_qg, z_hi, 0),
    ):
        pl.loop(1, HEADS)(lambda step: send_head(which, rem(head + step, HEADS), False))
        send_head(which, head, True)

    own = kv.at[:, 1:3, :, TILE : TILE + COLS, :]
    wait_bytes(own, recv_kv)

    after = worker(rem(x + 1, 4), head, quarter)
    before = worker(rem(x + 3, 4), head, quarter)
    mine = slice(TILE, TILE + COLS)
    hi, lo = slice(2 * TILE, 3 * TILE), slice(TILE, 2 * TILE)
    top, bottom = slice(3 * TILE, 4 * TILE), slice(0, TILE)

    def halo(n, src, dst, device):
        return copy_to(src, dst, send_n.at[n], recv_n.at[n], device)

    def side_halos(n, slabs, action):
        to_right, to_left = kv.at[:, slabs, :, hi, :], kv.at[:, slabs, :, lo, :]
        at_right, at_left = kv.at[:, slabs, :, bottom, :], kv.at[:, slabs, :, top, :]

        def send(k, src, dst, to):
            copy = copy_to(src, dst, send_n.at[n + k], recv_n.at[n + k % 2], worker(x, head, to))
            getattr(copy, action)()

        @pl.when(quarter < 3)
        def _():
            send(0, to_right, at_right, rem(quarter + 1, 4))

        @pl.when(quarter > 0)
        def _():
            send(1, to_left, at_left, rem(quarter + 3, 4))

        @pl.when(quarter == 1)
        def _():
            send(2, to_right, at_right, quarter - 1)

        @pl.when(quarter == 2)
        def _():
            send(3, to_left, at_left, quarter + 1)

        if action == "wait_send":
            wait_bytes(at_right, recv_n.at[n])
            wait_bytes(at_left, recv_n.at[n + 1])

    forward = halo(0, kv.at[:, 2, :, mine, :], kv.at[:, 0, :, mine, :], after)
    backward = halo(1, kv.at[:, 1, :, mine, :], kv.at[:, 3, :, mine, :], before)
    forward.start()
    backward.start()
    inner = slice(1, 3)
    side_halos(2, inner, "start")
    forward.wait_recv()
    side_halos(6, 0, "start")
    backward.wait_recv()
    side_halos(10, 3, "start")
    side_halos(2, inner, "wait_send")
    side_halos(6, 0, "wait_send")
    side_halos(10, 3, "wait_send")
    forward.wait_send()
    backward.wait_send()
    wait_bytes(qg, recv_qg)
    own_parts = sum(
        (part_place(k)[1] == quarter).astype(jnp.int32) for k in range(3)
    )
    for count in range(4):

        @pl.when(own_parts == count)
        def _():
            sent = kv.at[:, 0, :, 0 : SPAN - 16 * count, :]
            wait_bytes(sent, send_kv)
            wait_bytes(sent, send_qg)

    wait_bytes(kinds, kind_sems.at[1])

    @pl.when(jnp.logical_not(own_kind))
    def _():
        wait_bytes(flags, kind_sems.at[0])


def work_kernel(kinds, kv, qg, outs, dkv, acc):
    me = spot()
    along_time = kinds[0, 0] > 0
    step_t = jnp.where(along_time, 1, 0)
    acc[...] = jnp.zeros_like(acc)

    def one_tile(t, masked, slab, row, side):
        first = pl.multiple_of(side * TILE, 64)
        q = qg[0, slab, row, pl.ds(first, TILE), :]
        g = qg[1, slab, row, pl.ds(first, TILE), :]
        span = pl.ds(first, REACHED)
        where = []
        scores = []
        for n in range(3):
            s_at = jnp.where(along_time, slab + n, slab + 1)
            r_at = jnp.where(along_time, row, jnp.clip(row + n - 1, 0, 2))
            where.append((s_at, r_at))
            k_rows = kv[0, s_at, r_at, span, :]
            s = lax.dot_general(q, k_rows, (((1,), (1,)), ((), ())), preferred_element_type=jnp.float32)
            if masked:
                ok_time = jnp.logical_and(2 * me["x"] + slab + n - 1 >= 0, 2 * me["x"] + slab + n - 1 < 8)
                ok_row = jnp.logical_and(row + n - 1 >= 0, row + n - 1 < 3)
                ok = jnp.where(along_time, ok_time.astype(jnp.int32), ok_row.astype(jnp.int32))
                column = 2 * me["quarter"] + side
                low = jnp.where(column > 0, 0, TILE)
                high = jnp.where(column < 7, REACHED, 2 * TILE) * ok
                lane = lax.broadcasted_iota(jnp.int32, s.shape, 1)
                s = jnp.where(jnp.logical_and(lane >= low, lane < high), s, NEG_FILL)
            scores.append(s)
        top = jnp.max(jnp.maximum(jnp.maximum(scores[0], scores[1]), scores[2]), axis=1, keepdims=True)
        raised = [jnp.exp((s - top) * SCALE) for s in scores]
        total = jnp.sum(raised[0] + raised[1] + raised[2], axis=1, keepdims=True)
        share = 1.0 / total
        weights = [(r * share).astype(jnp.bfloat16) for r in raised]
        attended = jnp.zeros((TILE, DH), jnp.float32)
        for n in range(3):
            v_rows = kv[1, where[n][0], where[n][1], span, :]
            attended += jnp.dot(weights[n], v_rows, preferred_element_type=jnp.float32)
        attended = attended.astype(jnp.bfloat16)
        outs[0, slab, row, pl.ds(first, TILE), :] = attended
        delta = jnp.sum(g.astype(jnp.float32) * attended.astype(jnp.float32), axis=1, keepdims=True)
        q_grad = jnp.zeros((TILE, DH), jnp.float32)
        for n in range(3):
            s_at, r_at = where[n]
            v_rows = kv[1, s_at, r_at, span, :]
            w_grad = lax.dot_general(g, v_rows, (((1,), (1,)), ((), ())), preferred_element_type=jnp.float32)
            s_grad = (weights[n].astype(jnp.float32) * (w_grad - delta) * SCALE).astype(jnp.bfloat16)
            k_rows = kv[0, s_at, r_at, span, :]
            q_grad += jnp.dot(s_grad, k_rows, preferred_element_type=jnp.float32)
            acc[0, s_at, r_at, span, :] += lax.dot_general(
                s_grad, q, (((0,), (0,)), ((), ())), preferred_element_type=jnp.float32
            )
            acc[1, s_at, r_at, span, :] += lax.dot_general(
                weights[n], g, (((0,), (0,)), ((), ())), preferred_element_type=jnp.float32
            )
        outs[1, slab, row, pl.ds(first, TILE), :] = q_grad.astype(jnp.bfloat16)

    @pl.loop(0, 12)
    def _(t):
        slab, row, side = div(t, 6), rem(div(t, 2), 3), rem(t, 2)
        column = 2 * me["quarter"] + side
        slab_at = 2 * me["x"] + slab
        inside = jnp.where(
            along_time,
            jnp.logical_and(slab_at > 0, slab_at < 7).astype(jnp.int32),
            (row == 1).astype(jnp.int32),
        )
        full = jnp.logical_and(inside == 1, jnp.logical_and(column > 0, column < 7))

        @pl.when(full)
        def _():
            one_tile(t, False, slab, row, side)

        @pl.when(jnp.logical_not(full))
        def _():
            one_tile(t, True, slab, row, side)

    for s_at in range(4):
        for r_at in range(3):
            for a in range(2):
                dkv[a, s_at, r_at] = acc[a, s_at, r_at].astype(jnp.bfloat16)


def scatter_kernel(
    outs, dkv, attended, q_grad, k_grad, v_grad, from_side, from_slab, summed, final,
    send_o, recv_o, send_d, recv_d, send_n, recv_n
):
    me = spot()
    x, head, quarter = me["x"], me["head"], me["quarter"]
    greet(me)

    def send_parts(src_of, targets, send, recv):
        @pl.loop(0, 48)
        def _(step):
            n = rem(step + 3 * head, 48)
            slab, row, side, part = div(n, 24), div(rem(n, 24), 8), rem(div(n, 4), 2), rem(n, 4)
            tile = row * 8 + 2 * quarter + side
            at = rem(tile, 12) * 4 + part
            core, sub, k = div(tile, 12), div(at, 3), rem(at, 3)
            ctx = x * 4 + slab * 2 + core
            self_part = jnp.logical_and(ctx == lax.axis_index("ctx"), sub == me["sub"])
            first = pl.multiple_of(side * TILE + part * PART, 16)
            for a in range(2):
                src = src_of(a, slab, row, pl.ds(first, PART))
                dst = targets[a].at[
                    pl.ds(pl.multiple_of(k * PART, 16), PART), pl.ds(pl.multiple_of(head * DH, DH), DH)
                ]

                @pl.when(self_part)
                def _():
                    pltpu.make_async_copy(src, dst, recv).start()

                @pl.when(jnp.logical_not(self_part))
                def _():
                    copy_to(src, dst, send, recv, (ctx, sub)).start()

    send_parts(lambda a, s, r, rows: outs.at[a, s, r, rows, :], (attended, q_grad), send_o, recv_o.at[0])

    right = worker(x, head, rem(quarter + 1, 4))
    left = worker(x, head, rem(quarter + 3, 4))
    to_left = copy_to(dkv.at[:, :, :, 0:TILE, :], from_side.at[1], send_n.at[1], recv_n.at[1], left)
    to_right = copy_to(
        dkv.at[:, :, :, 3 * TILE : 4 * TILE, :], from_side.at[0], send_n.at[0], recv_n.at[0], right
    )
    @pl.when(quarter > 0)
    def _():
        to_left.start()

    @pl.when(quarter < 3)
    def _():
        to_right.start()

    for side in range(2):
        has = quarter > 0 if side == 0 else quarter < 3
        here = slice((1 + side) * TILE, (2 + side) * TILE)
        there = slice(side * TILE, (1 + side) * TILE)

        @pl.when(has)
        def _():
            wait_bytes(from_side.at[side], recv_n.at[side])
            for a in range(2):
                for s in range(4):
                    summed[a, s, :, there, :] = (
                        dkv[a, s, :, here, :].astype(jnp.float32) + from_side[side, a, s].astype(jnp.float32)
                    ).astype(jnp.bfloat16)

        @pl.when(jnp.logical_not(has))
        def _():
            for a in range(2):
                for s in range(4):
                    summed[a, s, :, there, :] = dkv[a, s, :, here, :]

    after = worker(rem(x + 1, 4), head, quarter)
    before = worker(rem(x + 3, 4), head, quarter)
    to_after = copy_to(summed.at[:, 3], from_slab.at[0], send_n.at[2], recv_n.at[2], after)
    to_before = copy_to(summed.at[:, 0], from_slab.at[1], send_n.at[3], recv_n.at[3], before)

    @pl.when(x < 3)
    def _():
        to_after.start()

    @pl.when(x > 0)
    def _():
        to_before.start()

    for slab in range(2):
        has = x > 0 if slab == 0 else x < 3

        @pl.when(has)
        def _():
            wait_bytes(from_slab.at[slab], recv_n.at[2 + slab])
            for a in range(2):
                final[a, slab] = (
                    summed[a, 1 + slab].astype(jnp.float32) + from_slab[slab, a].astype(jnp.float32)
                ).astype(jnp.bfloat16)

        @pl.when(jnp.logical_not(has))
        def _():
            for a in range(2):
                final[a, slab] = summed[a, 1 + slab]

    send_parts(lambda a, s, r, rows: final.at[a, s, r, rows, :], (k_grad, v_grad), send_d, recv_d.at[0])

    @pl.when(quarter > 0)
    def _():
        to_left.wait_send()

    @pl.when(quarter < 3)
    def _():
        to_right.wait_send()

    @pl.when(x < 3)
    def _():
        to_after.wait_send()

    @pl.when(x > 0)
    def _():
        to_before.wait_send()

    def own_part(k):
        at = me["sub"] * 3 + k
        tile = me["core"] * 12 + div(at, 4)
        return (div(rem(tile, 8), 2) == quarter).astype(jnp.int32)

    own_parts = own_part(0) + own_part(1) + own_part(2)
    for count in range(4):

        @pl.when(own_parts == count)
        def _():
            sent = dkv.at[:, 0, :, 0 : SPAN - 16 * count, :]
            wait_bytes(sent, send_o)
            wait_bytes(sent, send_d)

    wait_bytes(outs, recv_o.at[0])
    wait_bytes(final, recv_d.at[0])


def place_kernel(*refs):
    sources, results, buffers, sems = refs[:4], refs[4:8], refs[8:12], refs[12]
    loads = [pltpu.make_async_copy(s, b, sems.at[n]) for n, (s, b) in enumerate(zip(sources, buffers))]
    stores = [pltpu.make_async_copy(b, r, sems.at[4 + n]) for n, (b, r) in enumerate(zip(buffers, results))]
    for c in loads:
        c.start()
    for load, store in zip(loads, stores):
        load.wait()
        store.start()
    for c in stores:
        c.wait()


def per_device(queries, keys, values, out_grad, key_tiles):
    ctx = lax.axis_index("ctx")
    own_slab = ctx // 2
    lists = key_tiles[0]
    along_time = jnp.any(jnp.logical_and(lists >= 0, lists // 24 != own_slab))
    flags = jnp.broadcast_to(along_time.astype(jnp.int32), (8, 128))

    anywhere = pl.BlockSpec(memory_space=pl.ANY)
    vmem = pl.BlockSpec(memory_space=pltpu.VMEM)
    kv, qg, kinds = pl.pallas_call(
        gather_kernel,
        name="gather_heads",
        out_shape=(
            jax.ShapeDtypeStruct((2, 4, 3, SPAN, DH), jnp.bfloat16),
            jax.ShapeDtypeStruct((2, 2, 3, COLS, DH), jnp.bfloat16),
            jax.ShapeDtypeStruct((8, 128), jnp.int32),
        ),
        in_specs=[anywhere] * 5,
        out_specs=(anywhere, anywhere, anywhere),
        scratch_shapes=[
            pltpu.SemaphoreType.DMA,
            pltpu.SemaphoreType.DMA,
            pltpu.SemaphoreType.DMA,
            pltpu.SemaphoreType.DMA,
            pltpu.SemaphoreType.DMA((14,)),
            pltpu.SemaphoreType.DMA((14,)),
            pltpu.SemaphoreType.DMA((2,)),
        ],
        compiler_params=pltpu.CompilerParams(has_side_effects=True, collective_id=0),
    )(keys, values, queries, out_grad, flags)

    outs, dkv = pl.pallas_call(
        work_kernel,
        name="tile_attention",
        out_shape=(
            jax.ShapeDtypeStruct((2, 2, 3, COLS, DH), jnp.bfloat16),
            jax.ShapeDtypeStruct((2, 4, 3, SPAN, DH), jnp.bfloat16),
        ),
        in_specs=[pl.BlockSpec(memory_space=pltpu.SMEM), vmem, vmem],
        out_specs=(vmem, vmem),
        scratch_shapes=[pltpu.VMEM((2, 4, 3, SPAN, DH), jnp.float32)],
        compiler_params=pltpu.CompilerParams(vmem_limit_bytes=VMEM_LIMIT),
    )(kinds, kv, qg)

    token_block = jax.ShapeDtypeStruct((ROWS, HEADS * DH), jnp.bfloat16)
    blocks = pl.pallas_call(
        scatter_kernel,
        name="scatter_heads",
        out_shape=(token_block,) * 4,
        in_specs=[anywhere, vmem],
        out_specs=(anywhere,) * 4,
        scratch_shapes=[
            pltpu.VMEM((2, 2, 4, 3, TILE, DH), jnp.bfloat16),
            pltpu.VMEM((2, 2, 3, COLS, DH), jnp.bfloat16),
            pltpu.VMEM((2, 4, 3, COLS, DH), jnp.bfloat16),
            pltpu.VMEM((2, 2, 3, COLS, DH), jnp.bfloat16),
            pltpu.SemaphoreType.DMA,
            pltpu.SemaphoreType.DMA((1,)),
            pltpu.SemaphoreType.DMA,
            pltpu.SemaphoreType.DMA((1,)),
            pltpu.SemaphoreType.DMA((4,)),
            pltpu.SemaphoreType.DMA((4,)),
        ],
        compiler_params=pltpu.CompilerParams(has_side_effects=True, collective_id=1, vmem_limit_bytes=VMEM_LIMIT),
    )(outs, dkv)
    return pl.pallas_call(
        place_kernel,
        name="place_results",
        out_shape=(token_block,) * 4,
        in_specs=[anywhere] * 4,
        out_specs=(anywhere,) * 4,
        scratch_shapes=[pltpu.VMEM((ROWS, HEADS * DH), jnp.bfloat16)] * 4 + [pltpu.SemaphoreType.DMA((8,))],
        compiler_params=pltpu.CompilerParams(vmem_limit_bytes=VMEM_LIMIT),
    )(*blocks)


def solution(mesh):
    token_spec = P(("ctx", "head"), None)
    return jax.shard_map(
        per_device,
        mesh=mesh,
        in_specs=(token_spec,) * 4 + (P("head", "ctx", None),),
        out_specs=(token_spec,) * 4,
        check_vma=False,
    )
```

```python
import math

import jax
import jax.numpy as jnp
from jax import lax
from jax.experimental import pallas as pl
from jax.experimental.pallas import tpu as pltpu
from jax.sharding import PartitionSpec as P

DH = 128
TILE = 192
HEADS = 16
PART = 48
ROWS = 144
COLS = 2 * TILE
SPAN = 4 * TILE
REACHED = 3 * TILE
NEG_FILL = -1e30
SCALE = 1.0 / math.sqrt(DH)
LOG2E = 1.0 / math.log(2.0)
MESH = pl.DeviceIdType.MESH
VMEM_LIMIT = 60 * 1024 * 1024


def div(a, b):
    return lax.div(a, jnp.int32(b))


def rem(a, b):
    return lax.rem(a, jnp.int32(b))


def spot():
    ctx, sub = lax.axis_index("ctx"), lax.axis_index("head")
    core, z_hi, x = rem(ctx, 2), rem(div(ctx, 2), 2), div(ctx, 4)
    y, z_lo = rem(sub, 4), div(sub, 4)
    z = z_hi * 4 + z_lo
    head = 2 * z + div(y, 2)
    quarter = 2 * rem(y, 2) + core
    return dict(x=x, y=y, z=z, z_hi=z_hi, sub=sub, core=core, head=head, quarter=quarter)


def worker(x, head, quarter):
    z = div(head, 2)
    y = 2 * rem(head, 2) + div(quarter, 2)
    return (x * 4 + div(z, 4) * 2 + rem(quarter, 2), rem(z, 4) * 4 + y)


def copy_to(src, dst, send, recv, device):
    return pltpu.make_async_remote_copy(
        src_ref=src, dst_ref=dst, send_sem=send, recv_sem=recv, device_id=device, device_id_type=MESH
    )


def greet(me):
    barrier = pltpu.get_barrier_semaphore()
    x = me["x"]
    own = me["sub"] * 4 + me["z_hi"] * 2 + me["core"]

    @pl.loop(1, 64)
    def _(step):
        other = rem(own + step, 64)
        device = (x * 4 + rem(other, 4), div(other, 4))
        pl.semaphore_signal(barrier, inc=1, device_id=device, device_id_type=MESH)

    here = me["z_hi"] * 2 + me["core"]
    for step in (1, 3):
        device = (rem(x + step, 4) * 4 + here, me["sub"])
        pl.semaphore_signal(barrier, inc=1, device_id=device, device_id_type=MESH)
    pl.semaphore_wait(barrier, 65)


def wait_bytes(ref, sem):
    pltpu.make_async_copy(ref, ref, sem).wait()


def step_kernel(
    keys, queries, values, grads, flags,
    attended, q_grad, k_grad, v_grad,
    k, q, v, g, weights, group_grads, outs, dkv, from_side, from_slab, summed, final, kinds, kind,
    send_in, recv_in, halo_send, halo_recv, kind_sems, send_out, recv_out, side_send, side_recv, slab_send, slab_recv
):
    me = spot()
    x, z_hi, core, head, quarter = me["x"], me["z_hi"], me["core"], me["head"], me["quarter"]
    flip = rem(div(head, 2), 2)
    swap = rem(head, 2)

    def row_of(place):
        return place + flip * (2 - 2 * place)

    def part_place(n):
        at = me["sub"] * 3 + n
        tile = core * 12 + div(at, 4)
        column = rem(tile, 8)
        return div(tile, 8), div(column, 2), rem(column, 2), rem(at, 4)

    own_parts = sum((part_place(n)[1] == quarter).astype(jnp.int32) for n in range(3))

    greet(me)

    def send_head(n, target_head, own_head):
        source, out, slab, shift = inputs[n]
        for part_n in range(3):
            row, to, side, part = part_place(part_n)
            first = pl.multiple_of((side + shift) * TILE + part * PART, 16)
            src = source.at[pl.ds(part_n * PART, PART), pl.ds(pl.multiple_of(target_head * DH, DH), DH)]
            dst = out.at[slab, row, pl.ds(first, PART), :]
            remote = copy_to(src, dst, send_in.at[n], recv_in.at[n], worker(x, target_head, to))
            if own_head:

                @pl.when(to == quarter)
                def _():
                    pltpu.make_async_copy(src, dst, recv_in.at[n]).start()

                @pl.when(to != quarter)
                def _():
                    remote.start()

            else:
                remote.start()

    inputs = ((keys, k, 1 + z_hi, 1), (queries, q, z_hi, 0), (values, v, 1 + z_hi, 1), (grads, g, z_hi, 0))

    asker = (
        x * 4 + div(me["sub"], 8) * 2 + core,
        rem(div(me["sub"], 2), 4) * 4 + 2 * rem(me["sub"], 2) + z_hi,
    )
    own_kind = jnp.logical_and(me["sub"] == head, rem(me["y"], 2) == z_hi)

    @pl.when(own_kind)
    def _():
        pltpu.make_async_copy(flags, kinds, kind_sems.at[1]).start()

    @pl.when(jnp.logical_not(own_kind))
    def _():
        copy_to(flags, kinds, kind_sems.at[0], kind_sems.at[1], asker).start()

    for n in range(4):
        pl.loop(1, HEADS)(lambda step: send_head(n, rem(head + step, HEADS), False))
        send_head(n, head, True)

    for a in range(2):
        group_grads[a, 18] = jnp.zeros((SPAN, DH), jnp.float32)

    mine = slice(TILE, TILE + COLS)
    hi, lo = slice(2 * TILE, 3 * TILE), slice(TILE, 2 * TILE)
    top, bottom = slice(3 * TILE, 4 * TILE), slice(0, TILE)
    after = worker(rem(x + 1, 4), head, quarter)
    before = worker(rem(x + 3, 4), head, quarter)

    class Halo:
        def __init__(self, buf, base):
            self.buf, self.base = buf, base
            self.forward = copy_to(
                buf.at[2, :, mine, :], buf.at[0, :, mine, :], halo_send.at[base], halo_recv.at[base], after
            )
            self.backward = copy_to(
                buf.at[1, :, mine, :], buf.at[3, :, mine, :], halo_send.at[base + 1], halo_recv.at[base + 1], before
            )

        def sides(self, n, slabs, action):
            buf, n = self.buf, self.base + n
            to_right, to_left = buf.at[slabs, :, hi, :], buf.at[slabs, :, lo, :]
            at_right, at_left = buf.at[slabs, :, bottom, :], buf.at[slabs, :, top, :]

            def send(j, src, dst, to):
                copy = copy_to(src, dst, halo_send.at[n + j], halo_recv.at[n + j % 2], worker(x, head, to))
                getattr(copy, action)()

            @pl.when(quarter < 3)
            def _():
                send(0, to_right, at_right, rem(quarter + 1, 4))

            @pl.when(quarter > 0)
            def _():
                send(1, to_left, at_left, rem(quarter + 3, 4))

            @pl.when(quarter == 1)
            def _():
                send(2, to_right, at_right, quarter - 1)

            @pl.when(quarter == 2)
            def _():
                send(3, to_left, at_left, quarter + 1)

            if action == "wait_send":
                wait_bytes(at_right, halo_recv.at[n])
                wait_bytes(at_left, halo_recv.at[n + 1])

        def begin(self):
            self.forward.start()
            self.backward.start()
            self.sides(2, slice(1, 3), "start")

        def go_on(self):
            self.forward.wait_recv()
            self.sides(6, 0, "start")
            self.backward.wait_recv()
            self.sides(10, 3, "start")

        def end(self):
            self.sides(2, slice(1, 3), "wait_send")
            self.sides(6, 0, "wait_send")
            self.sides(10, 3, "wait_send")
            self.forward.wait_send()
            self.backward.wait_send()

    key_halo, value_halo = Halo(k, 0), Halo(v, 14)
    wait_bytes(k.at[1:3, :, mine, :], recv_in.at[0])
    key_halo.begin()
    key_halo.go_on()
    wait_bytes(kinds, kind_sems.at[1])
    to_scalar = pltpu.make_async_copy(kinds, kind, kind_sems.at[2])
    to_scalar.start()
    to_scalar.wait()
    along_time = kind[0, 0]
    key_halo.end()
    wait_bytes(q, recv_in.at[1])

    def group_at(n, slab, row):
        return (
            jnp.where(along_time > 0, slab + n, slab + 1),
            jnp.where(along_time > 0, row, jnp.clip(row + n - 1, 0, 2)),
        )

    def places(step):
        return rem(step + swap, 2), row_of(div(step, 2))

    @pl.loop(0, 6)
    def _(step):
        @pl.when(step == 3)
        def _():
            wait_bytes(v.at[1:3, :, mine, :], recv_in.at[2])
            value_halo.begin()

        slab, row = places(step)
        lane = lax.broadcasted_iota(jnp.int32, (1, REACHED), 1)
        for side in range(2):
            rows = q[slab, row, side * TILE : (side + 1) * TILE, :]
            column = 2 * quarter + side
            low = jnp.where(column > 0, 0, TILE)
            high = jnp.where(column < 7, REACHED, 2 * TILE)
            scores = []
            for n in range(3):
                s_at, r_at = group_at(n, slab, row)
                k_rows = k[s_at, r_at, side * TILE : side * TILE + REACHED, :]
                s = lax.dot_general(rows, k_rows, (((1,), (1,)), ((), ())), preferred_element_type=jnp.float32)
                slab_in = 2 * x + slab + n - 1
                ok_time = jnp.logical_and(slab_in >= 0, slab_in < 8).astype(jnp.int32)
                ok_row = jnp.logical_and(row + n - 1 >= 0, row + n - 1 < 3).astype(jnp.int32)
                last = high * jnp.where(along_time > 0, ok_time, ok_row)
                s = s + jnp.where(jnp.logical_and(lane >= low, lane < last), 0.0, NEG_FILL)
                scores.append(s)
            peak = jnp.max(jnp.maximum(jnp.maximum(scores[0], scores[1]), scores[2]), axis=1, keepdims=True)
            raised = [jnp.exp2((s - peak) * (SCALE * LOG2E)) for s in scores]
            share = 1.0 / jnp.sum(raised[0] + raised[1] + raised[2], axis=1, keepdims=True)
            for n in range(3):
                weights[step, side, n] = (raised[n] * share).astype(jnp.bfloat16)

    value_halo.go_on()
    value_halo.end()
    wait_bytes(g, recv_in.at[3])

    def send_part(slab, row, side, part, source, targets, send, recv):
        tile = row * 8 + 2 * quarter + side
        at = rem(tile, 12) * 4 + part
        to_core, sub, n = div(tile, 12), div(at, 3), rem(at, 3)
        ctx = x * 4 + slab * 2 + to_core
        self_part = jnp.logical_and(ctx == lax.axis_index("ctx"), sub == me["sub"])
        first = pl.multiple_of(side * TILE + part * PART, 16)
        for a in range(2):
            src = source.at[a, slab, row, pl.ds(first, PART), :]
            dst = targets[a].at[pl.ds(pl.multiple_of(n * PART, 16), PART), pl.ds(pl.multiple_of(head * DH, DH), DH)]

            @pl.when(self_part)
            def _():
                pltpu.make_async_copy(src, dst, recv).start()

            @pl.when(jnp.logical_not(self_part))
            def _():
                copy_to(src, dst, send, recv, (ctx, sub)).start()

    def side_copies(place):
        row = row_of(place)
        left = worker(x, head, rem(quarter + 3, 4))
        right = worker(x, head, rem(quarter + 1, 4))
        return (
            copy_to(
                dkv.at[:, :, row, top, :], from_side.at[0, :, :, row], side_send.at[0, place], side_recv.at[0, place], right
            ),
            copy_to(
                dkv.at[:, :, row, bottom, :], from_side.at[1, :, :, row], side_send.at[1, place], side_recv.at[1, place], left
            ),
        )

    def gather_groups(place):
        row = row_of(place)
        for s_at in range(4):
            if 1 <= s_at <= 2:
                same = 6 + (s_at - 1) * 3 + row
                previous = jnp.where(
                    along_time > 0,
                    s_at * 3 + row if s_at < 2 else 18,
                    jnp.where(row < 2, (s_at - 1) * 3 + row + 1, 18),
                )
                following = jnp.where(
                    along_time > 0,
                    12 + (s_at - 2) * 3 + row if s_at >= 2 else 18,
                    jnp.where(row > 0, 12 + (s_at - 1) * 3 + row - 1, 18),
                )
                for a in range(2):
                    total = group_grads[a, same] + group_grads[a, previous] + group_grads[a, following]
                    dkv[a, s_at, row] = total.astype(jnp.bfloat16)
            else:
                only = jnp.where(along_time > 0, row if s_at == 0 else 15 + row, 18)
                for a in range(2):
                    dkv[a, s_at, row] = group_grads[a, only].astype(jnp.bfloat16)
        to_right, to_left = side_copies(place)

        @pl.when(quarter < 3)
        def _():
            to_right.start()

        @pl.when(quarter > 0)
        def _():
            to_left.start()

    @pl.loop(0, 6)
    def _(step):
        slab, row = places(step)
        parts = []
        for side in range(2):
            here = slice(side * TILE, (side + 1) * TILE)
            span = slice(side * TILE, side * TILE + REACHED)
            q_rows, g_rows = q[slab, row, here, :], g[slab, row, here, :]
            attend = jnp.zeros((TILE, DH), jnp.float32)
            for n in range(3):
                s_at, r_at = group_at(n, slab, row)
                attend += jnp.dot(weights[step, side, n], v[s_at, r_at, span, :], preferred_element_type=jnp.float32)
            attend = attend.astype(jnp.bfloat16)
            outs[0, slab, row, here, :] = attend
            delta = jnp.sum(g_rows.astype(jnp.float32) * attend.astype(jnp.float32), axis=1, keepdims=True)
            q_sum = jnp.zeros((TILE, DH), jnp.float32)
            for n in range(3):
                s_at, r_at = group_at(n, slab, row)
                w = weights[step, side, n]
                w_grad = lax.dot_general(
                    g_rows, v[s_at, r_at, span, :], (((1,), (1,)), ((), ())), preferred_element_type=jnp.float32
                )
                s_grad = (w.astype(jnp.float32) * (w_grad - delta) * SCALE).astype(jnp.bfloat16)
                q_sum += jnp.dot(s_grad, k[s_at, r_at, span, :], preferred_element_type=jnp.float32)
                block = n * 6 + slab * 3 + row
                for a, left_side, right_side in ((0, s_grad, q_rows), (1, w, g_rows)):
                    piece = lax.dot_general(
                        left_side, right_side, (((0,), (0,)), ((), ())), preferred_element_type=jnp.float32
                    )
                    if side == 0:
                        group_grads[a, block, 0:REACHED] = piece
                    else:
                        group_grads[a, block, TILE:REACHED] += piece[0 : 2 * TILE]
                        group_grads[a, block, REACHED:SPAN] = piece[2 * TILE :]
            outs[1, slab, row, here, :] = q_sum.astype(jnp.bfloat16)

        @pl.loop(0, 8)
        def _(n):
            at = rem(n + 3 * head, 8)
            send_part(slab, row, div(at, 4), rem(at, 4), outs, (attended, q_grad), send_out.at[0], recv_out.at[0])

        @pl.when(step == 3)
        def _():
            gather_groups(0)

    gather_groups(1)
    gather_groups(2)

    def slab_copies(place):
        row = row_of(place)
        return (
            copy_to(summed.at[:, 3, row], from_slab.at[0, :, row], slab_send.at[0, place], slab_recv.at[0, place], after),
            copy_to(summed.at[:, 0, row], from_slab.at[1, :, row], slab_send.at[1, place], slab_recv.at[1, place], before),
        )

    for place in range(3):
        row = row_of(place)
        for side in range(2):
            has = quarter > 0 if side == 0 else quarter < 3
            here = slice((1 + side) * TILE, (2 + side) * TILE)
            there = slice(side * TILE, (1 + side) * TILE)

            @pl.when(has)
            def _():
                wait_bytes(from_side.at[side, :, :, row], side_recv.at[side, place])
                for a in range(2):
                    for s in range(4):
                        summed[a, s, row, there, :] = (
                            dkv[a, s, row, here, :].astype(jnp.float32) + from_side[side, a, s, row].astype(jnp.float32)
                        ).astype(jnp.bfloat16)

            @pl.when(jnp.logical_not(has))
            def _():
                for a in range(2):
                    for s in range(4):
                        summed[a, s, row, there, :] = dkv[a, s, row, here, :]

        to_after, to_before = slab_copies(place)

        @pl.when(x < 3)
        def _():
            to_after.start()

        @pl.when(x > 0)
        def _():
            to_before.start()

    for place in range(3):
        row = row_of(place)
        for slab in range(2):
            has = x > 0 if slab == 0 else x < 3

            @pl.when(has)
            def _():
                wait_bytes(from_slab.at[slab, :, row], slab_recv.at[slab, place])
                for a in range(2):
                    final[a, slab, row] = (
                        summed[a, 1 + slab, row].astype(jnp.float32) + from_slab[slab, a, row].astype(jnp.float32)
                    ).astype(jnp.bfloat16)

            @pl.when(jnp.logical_not(has))
            def _():
                for a in range(2):
                    final[a, slab, row] = summed[a, 1 + slab, row]

        @pl.loop(0, 16)
        def _(n):
            at = rem(n + 3 * head, 16)
            send_part(
                div(at, 8), row, rem(div(at, 4), 2), rem(at, 4), final, (k_grad, v_grad), send_out.at[1], recv_out.at[1]
            )

    for place in range(3):
        to_right, to_left = side_copies(place)
        to_after, to_before = slab_copies(place)
        for has, copy in ((quarter < 3, to_right), (quarter > 0, to_left), (x < 3, to_after), (x > 0, to_before)):

            @pl.when(has)
            def _():
                copy.wait_send()

    for count in range(4):

        @pl.when(own_parts == count)
        def _():
            for n in range(4):
                wait_bytes(k.at[0, :, 0 : SPAN - 16 * count, :], send_in.at[n])
            for n in range(2):
                wait_bytes(dkv.at[:, 0, :, 0 : SPAN - 16 * count, :], send_out.at[n])

    @pl.when(jnp.logical_not(own_kind))
    def _():
        wait_bytes(flags, kind_sems.at[0])

    wait_bytes(outs, recv_out.at[0])
    wait_bytes(final, recv_out.at[1])


def place_kernel(*refs):
    sources, results, buffers, sems = refs[:4], refs[4:8], refs[8:12], refs[12]
    loads = [pltpu.make_async_copy(s, b, sems.at[n]) for n, (s, b) in enumerate(zip(sources, buffers))]
    stores = [pltpu.make_async_copy(b, r, sems.at[4 + n]) for n, (b, r) in enumerate(zip(buffers, results))]
    for c in loads:
        c.start()
    for load, store in zip(loads, stores):
        load.wait()
        store.start()
    for c in stores:
        c.wait()


def per_device(queries, keys, values, out_grad, key_tiles):
    ctx = lax.axis_index("ctx")
    own_slab = ctx // 2
    lists = key_tiles[0]
    along_time = jnp.any(jnp.logical_and(lists >= 0, lists // 24 != own_slab))
    flags = jnp.broadcast_to(along_time.astype(jnp.int32), (8, 128))

    anywhere = pl.BlockSpec(memory_space=pl.ANY)
    token_block = jax.ShapeDtypeStruct((ROWS, HEADS * DH), jnp.bfloat16)
    near = pltpu.VMEM((4, 3, SPAN, DH), jnp.bfloat16)
    own = pltpu.VMEM((2, 3, COLS, DH), jnp.bfloat16)
    pair = pltpu.VMEM((2, 2, 3, COLS, DH), jnp.bfloat16)
    blocks = pl.pallas_call(
        step_kernel,
        name="attention_step",
        out_shape=(token_block,) * 4,
        in_specs=[anywhere] * 5,
        out_specs=(anywhere,) * 4,
        scratch_shapes=[
            near,
            own,
            near,
            own,
            pltpu.VMEM((6, 2, 3, TILE, REACHED), jnp.bfloat16),
            pltpu.VMEM((2, 19, SPAN, DH), jnp.float32),
            pair,
            pltpu.VMEM((2, 4, 3, SPAN, DH), jnp.bfloat16),
            pltpu.VMEM((2, 2, 4, 3, TILE, DH), jnp.bfloat16),
            pair,
            pltpu.VMEM((2, 4, 3, COLS, DH), jnp.bfloat16),
            pair,
            pltpu.VMEM((8, 128), jnp.int32),
            pltpu.SMEM((8, 128), jnp.int32),
            pltpu.SemaphoreType.DMA((4,)),
            pltpu.SemaphoreType.DMA((4,)),
            pltpu.SemaphoreType.DMA((28,)),
            pltpu.SemaphoreType.DMA((28,)),
            pltpu.SemaphoreType.DMA((3,)),
            pltpu.SemaphoreType.DMA((2,)),
            pltpu.SemaphoreType.DMA((2,)),
            pltpu.SemaphoreType.DMA((2, 3)),
            pltpu.SemaphoreType.DMA((2, 3)),
            pltpu.SemaphoreType.DMA((2, 3)),
            pltpu.SemaphoreType.DMA((2, 3)),
        ],
        compiler_params=pltpu.CompilerParams(has_side_effects=True, collective_id=0, vmem_limit_bytes=VMEM_LIMIT),
    )(keys, queries, values, out_grad, flags)
    return pl.pallas_call(
        place_kernel,
        name="place_results",
        out_shape=(token_block,) * 4,
        in_specs=[anywhere] * 4,
        out_specs=(anywhere,) * 4,
        scratch_shapes=[pltpu.VMEM((ROWS, HEADS * DH), jnp.bfloat16)] * 4 + [pltpu.SemaphoreType.DMA((8,))],
        compiler_params=pltpu.CompilerParams(vmem_limit_bytes=VMEM_LIMIT),
    )(*blocks)


def solution(mesh):
    token_spec = P(("ctx", "head"), None)
    return jax.shard_map(
        per_device,
        mesh=mesh,
        in_specs=(token_spec,) * 4 + (P("head", "ctx", None),),
        out_specs=(token_spec,) * 4,
        check_vma=False,
    )
```

```python
import math

import jax
import jax.numpy as jnp
from jax import lax
from jax.experimental import pallas as pl
from jax.experimental.pallas import tpu as pltpu
from jax.sharding import PartitionSpec as P

DH = 128
TILE = 192
HEADS = 16
PART = 48
ROWS = 144
COLS = 2 * TILE
SPAN = 4 * TILE
REACHED = 3 * TILE
NEG_FILL = -1e30
SCALE = 1.0 / math.sqrt(DH)
LOG2E = 1.0 / math.log(2.0)
MESH = pl.DeviceIdType.MESH
VMEM_LIMIT = 60 * 1024 * 1024


def div(a, b):
    return lax.div(a, jnp.int32(b))


def rem(a, b):
    return lax.rem(a, jnp.int32(b))


def spot():
    ctx, sub = lax.axis_index("ctx"), lax.axis_index("head")
    core, z_hi, x = rem(ctx, 2), rem(div(ctx, 2), 2), div(ctx, 4)
    y, z_lo = rem(sub, 4), div(sub, 4)
    z = z_hi * 4 + z_lo
    head = 2 * z + div(y, 2)
    quarter = 2 * rem(y, 2) + core
    return dict(x=x, y=y, z=z, z_hi=z_hi, sub=sub, core=core, head=head, quarter=quarter)


def worker(x, head, quarter):
    z = div(head, 2)
    y = 2 * rem(head, 2) + div(quarter, 2)
    return (x * 4 + div(z, 4) * 2 + rem(quarter, 2), rem(z, 4) * 4 + y)


def copy_to(src, dst, send, recv, device):
    return pltpu.make_async_remote_copy(
        src_ref=src, dst_ref=dst, send_sem=send, recv_sem=recv, device_id=device, device_id_type=MESH
    )


def greet(me):
    barrier = pltpu.get_barrier_semaphore()
    x = me["x"]
    own = me["sub"] * 4 + me["z_hi"] * 2 + me["core"]

    @pl.loop(1, 64)
    def _(step):
        other = rem(own + step, 64)
        device = (x * 4 + rem(other, 4), div(other, 4))
        pl.semaphore_signal(barrier, inc=1, device_id=device, device_id_type=MESH)

    here = me["z_hi"] * 2 + me["core"]
    for step in (1, 3):
        device = (rem(x + step, 4) * 4 + here, me["sub"])
        pl.semaphore_signal(barrier, inc=1, device_id=device, device_id_type=MESH)
    pl.semaphore_wait(barrier, 65)


def wait_bytes(ref, sem):
    pltpu.make_async_copy(ref, ref, sem).wait()


def step_kernel(
    keys, queries, values, grads, flags,
    attended, q_grad, k_grad, v_grad,
    k, q, v, g, weights, group_grads, outs, dkv, from_side, from_slab, summed, final, kinds, kind,
    send_in, recv_in, halo_send, halo_recv, kind_sems, send_out, recv_out, side_send, side_recv, slab_send, slab_recv
):
    me = spot()
    x, z_hi, core, head, quarter = me["x"], me["z_hi"], me["core"], me["head"], me["quarter"]
    flip = rem(div(head, 2), 2)
    swap = rem(head, 2)

    def row_of(place):
        return place + flip * (2 - 2 * place)

    def part_place(n):
        at = me["sub"] * 3 + n
        tile = core * 12 + div(at, 4)
        column = rem(tile, 8)
        return div(tile, 8), div(column, 2), rem(column, 2), rem(at, 4)

    own_parts = sum((part_place(n)[1] == quarter).astype(jnp.int32) for n in range(3))

    greet(me)

    def send_head(n, target_head, own_head):
        source, out, slab, shift = inputs[n]
        for part_n in range(3):
            row, to, side, part = part_place(part_n)
            first = pl.multiple_of((side + shift) * TILE + part * PART, 16)
            src = source.at[pl.ds(part_n * PART, PART), pl.ds(pl.multiple_of(target_head * DH, DH), DH)]
            dst = out.at[slab, row, pl.ds(first, PART), :]
            remote = copy_to(src, dst, send_in.at[n], recv_in.at[n], worker(x, target_head, to))
            if own_head:

                @pl.when(to == quarter)
                def _():
                    pltpu.make_async_copy(src, dst, recv_in.at[n]).start()

                @pl.when(to != quarter)
                def _():
                    remote.start()

            else:
                remote.start()

    inputs = ((keys, k, 1 + z_hi, 1), (queries, q, z_hi, 0), (values, v, 1 + z_hi, 1), (grads, g, z_hi, 0))

    asker = (
        x * 4 + div(me["sub"], 8) * 2 + core,
        rem(div(me["sub"], 2), 4) * 4 + 2 * rem(me["sub"], 2) + z_hi,
    )
    own_kind = jnp.logical_and(me["sub"] == head, rem(me["y"], 2) == z_hi)

    @pl.when(own_kind)
    def _():
        pltpu.make_async_copy(flags, kinds, kind_sems.at[1]).start()

    @pl.when(jnp.logical_not(own_kind))
    def _():
        copy_to(flags, kinds, kind_sems.at[0], kind_sems.at[1], asker).start()

    for n in range(4):
        pl.loop(1, HEADS)(lambda step: send_head(n, rem(head + step, HEADS), False))
        send_head(n, head, True)

    for a in range(2):
        group_grads[a, 18] = jnp.zeros((SPAN, DH), jnp.float32)

    mine = slice(TILE, TILE + COLS)
    hi, lo = slice(2 * TILE, 3 * TILE), slice(TILE, 2 * TILE)
    top, bottom = slice(3 * TILE, 4 * TILE), slice(0, TILE)
    after = worker(rem(x + 1, 4), head, quarter)
    before = worker(rem(x + 3, 4), head, quarter)

    class Halo:
        def __init__(self, buf, base):
            self.buf, self.base = buf, base
            self.forward = copy_to(
                buf.at[2, :, mine, :], buf.at[0, :, mine, :], halo_send.at[base], halo_recv.at[base], after
            )
            self.backward = copy_to(
                buf.at[1, :, mine, :], buf.at[3, :, mine, :], halo_send.at[base + 1], halo_recv.at[base + 1], before
            )

        def sides(self, n, slabs, action):
            buf, n = self.buf, self.base + n
            to_right, to_left = buf.at[slabs, :, hi, :], buf.at[slabs, :, lo, :]
            at_right, at_left = buf.at[slabs, :, bottom, :], buf.at[slabs, :, top, :]

            def send(j, src, dst, to):
                copy = copy_to(src, dst, halo_send.at[n + j], halo_recv.at[n + j % 2], worker(x, head, to))
                getattr(copy, action)()

            @pl.when(quarter < 3)
            def _():
                send(0, to_right, at_right, rem(quarter + 1, 4))

            @pl.when(quarter > 0)
            def _():
                send(1, to_left, at_left, rem(quarter + 3, 4))

            @pl.when(quarter == 1)
            def _():
                send(2, to_right, at_right, quarter - 1)

            @pl.when(quarter == 2)
            def _():
                send(3, to_left, at_left, quarter + 1)

            if action == "wait_send":
                wait_bytes(at_right, halo_recv.at[n])
                wait_bytes(at_left, halo_recv.at[n + 1])

        def begin(self):
            self.forward.start()
            self.backward.start()
            self.sides(2, slice(1, 3), "start")

        def go_on(self):
            self.forward.wait_recv()
            self.sides(6, 0, "start")
            self.backward.wait_recv()
            self.sides(10, 3, "start")

        def end(self):
            self.sides(2, slice(1, 3), "wait_send")
            self.sides(6, 0, "wait_send")
            self.sides(10, 3, "wait_send")
            self.forward.wait_send()
            self.backward.wait_send()

    key_halo, value_halo = Halo(k, 0), Halo(v, 14)
    wait_bytes(k.at[1:3, :, mine, :], recv_in.at[0])
    key_halo.begin()
    key_halo.go_on()
    wait_bytes(kinds, kind_sems.at[1])
    to_scalar = pltpu.make_async_copy(kinds, kind, kind_sems.at[2])
    to_scalar.start()
    to_scalar.wait()
    along_time = kind[0, 0]
    key_halo.end()
    wait_bytes(q, recv_in.at[1])

    def group_at(n, slab, row):
        return (
            jnp.where(along_time > 0, slab + n, slab + 1),
            jnp.where(along_time > 0, row, jnp.clip(row + n - 1, 0, 2)),
        )

    def places(step):
        return rem(step + swap, 2), row_of(div(step, 2))

    @pl.loop(0, 6)
    def _(step):
        @pl.when(step == 3)
        def _():
            wait_bytes(v.at[1:3, :, mine, :], recv_in.at[2])
            value_halo.begin()

        slab, row = places(step)
        lane = lax.broadcasted_iota(jnp.int32, (1, REACHED), 1)
        for side in range(2):
            rows = q[slab, row, side * TILE : (side + 1) * TILE, :]
            column = 2 * quarter + side
            low = jnp.where(column > 0, 0, TILE)
            high = jnp.where(column < 7, REACHED, 2 * TILE)
            scores = []
            for n in range(3):
                s_at, r_at = group_at(n, slab, row)
                k_rows = k[s_at, r_at, side * TILE : side * TILE + REACHED, :]
                s = lax.dot_general(rows, k_rows, (((1,), (1,)), ((), ())), preferred_element_type=jnp.float32)
                slab_in = 2 * x + slab + n - 1
                ok_time = jnp.logical_and(slab_in >= 0, slab_in < 8).astype(jnp.int32)
                ok_row = jnp.logical_and(row + n - 1 >= 0, row + n - 1 < 3).astype(jnp.int32)
                last = high * jnp.where(along_time > 0, ok_time, ok_row)
                s = s + jnp.where(jnp.logical_and(lane >= low, lane < last), 0.0, NEG_FILL)
                scores.append(s)
            peak = jnp.max(jnp.maximum(jnp.maximum(scores[0], scores[1]), scores[2]), axis=1, keepdims=True)
            raised = [jnp.exp2((s - peak) * (SCALE * LOG2E)) for s in scores]
            share = 1.0 / jnp.sum(raised[0] + raised[1] + raised[2], axis=1, keepdims=True)
            for n in range(3):
                weights[step, side, n] = (raised[n] * share).astype(jnp.bfloat16)

    value_halo.go_on()
    value_halo.end()
    wait_bytes(g, recv_in.at[3])

    def send_part(slab, row, side, part, source, targets, send, recv):
        tile = row * 8 + 2 * quarter + side
        at = rem(tile, 12) * 4 + part
        to_core, sub, n = div(tile, 12), div(at, 3), rem(at, 3)
        ctx = x * 4 + slab * 2 + to_core
        self_part = jnp.logical_and(ctx == lax.axis_index("ctx"), sub == me["sub"])
        first = pl.multiple_of(side * TILE + part * PART, 16)
        for a in range(2):
            src = source.at[a, slab, row, pl.ds(first, PART), :]
            dst = targets[a].at[pl.ds(pl.multiple_of(n * PART, 16), PART), pl.ds(pl.multiple_of(head * DH, DH), DH)]

            @pl.when(self_part)
            def _():
                pltpu.make_async_copy(src, dst, recv).start()

            @pl.when(jnp.logical_not(self_part))
            def _():
                copy_to(src, dst, send, recv, (ctx, sub)).start()

    def side_copies(place):
        row = row_of(place)
        left = worker(x, head, rem(quarter + 3, 4))
        right = worker(x, head, rem(quarter + 1, 4))
        return (
            copy_to(
                dkv.at[:, :, row, top, :], from_side.at[0, :, :, row], side_send.at[0, place], side_recv.at[0, place], right
            ),
            copy_to(
                dkv.at[:, :, row, bottom, :], from_side.at[1, :, :, row], side_send.at[1, place], side_recv.at[1, place], left
            ),
        )

    def gather_groups(place):
        row = row_of(place)
        for s_at in range(4):
            if 1 <= s_at <= 2:
                same = 6 + (s_at - 1) * 3 + row
                previous = jnp.where(
                    along_time > 0,
                    s_at * 3 + row if s_at < 2 else 18,
                    jnp.where(row < 2, (s_at - 1) * 3 + row + 1, 18),
                )
                following = jnp.where(
                    along_time > 0,
                    12 + (s_at - 2) * 3 + row if s_at >= 2 else 18,
                    jnp.where(row > 0, 12 + (s_at - 1) * 3 + row - 1, 18),
                )
                for a in range(2):
                    total = group_grads[a, same] + group_grads[a, previous] + group_grads[a, following]
                    dkv[a, s_at, row] = total.astype(jnp.bfloat16)
            else:
                only = jnp.where(along_time > 0, row if s_at == 0 else 15 + row, 18)
                for a in range(2):
                    dkv[a, s_at, row] = group_grads[a, only].astype(jnp.bfloat16)
        to_right, to_left = side_copies(place)

        @pl.when(quarter < 3)
        def _():
            to_right.start()

        @pl.when(quarter > 0)
        def _():
            to_left.start()

    def slab_copies(place):
        row = row_of(place)
        return (
            copy_to(summed.at[:, 3, row], from_slab.at[0, :, row], slab_send.at[0, place], slab_recv.at[0, place], after),
            copy_to(summed.at[:, 0, row], from_slab.at[1, :, row], slab_send.at[1, place], slab_recv.at[1, place], before),
        )

    def add_sides(place):
        row = row_of(place)
        for side in range(2):
            has = quarter > 0 if side == 0 else quarter < 3
            here = slice((1 + side) * TILE, (2 + side) * TILE)
            there = slice(side * TILE, (1 + side) * TILE)

            @pl.when(has)
            def _():
                wait_bytes(from_side.at[side, :, :, row], side_recv.at[side, place])
                for a in range(2):
                    for s in range(4):
                        summed[a, s, row, there, :] = (
                            dkv[a, s, row, here, :].astype(jnp.float32) + from_side[side, a, s, row].astype(jnp.float32)
                        ).astype(jnp.bfloat16)

            @pl.when(jnp.logical_not(has))
            def _():
                for a in range(2):
                    for s in range(4):
                        summed[a, s, row, there, :] = dkv[a, s, row, here, :]

        to_after, to_before = slab_copies(place)

        @pl.when(x < 3)
        def _():
            to_after.start()

        @pl.when(x > 0)
        def _():
            to_before.start()

    def finish(place):
        row = row_of(place)
        for slab in range(2):
            has = x > 0 if slab == 0 else x < 3

            @pl.when(has)
            def _():
                wait_bytes(from_slab.at[slab, :, row], slab_recv.at[slab, place])
                for a in range(2):
                    final[a, slab, row] = (
                        summed[a, 1 + slab, row].astype(jnp.float32) + from_slab[slab, a, row].astype(jnp.float32)
                    ).astype(jnp.bfloat16)

            @pl.when(jnp.logical_not(has))
            def _():
                for a in range(2):
                    final[a, slab, row] = summed[a, 1 + slab, row]

        @pl.loop(0, 16)
        def _(n):
            at = rem(n + 3 * head, 16)
            send_part(
                div(at, 8), row, rem(div(at, 4), 2), rem(at, 4), final, (k_grad, v_grad), send_out.at[1], recv_out.at[1]
            )

    @pl.loop(0, 6)
    def _(step):
        slab, row = places(step)
        for side in range(2):
            here = slice(side * TILE, (side + 1) * TILE)
            span = slice(side * TILE, side * TILE + REACHED)
            q_rows, g_rows = q[slab, row, here, :], g[slab, row, here, :]
            attend = jnp.zeros((TILE, DH), jnp.float32)
            for n in range(3):
                s_at, r_at = group_at(n, slab, row)
                attend += jnp.dot(weights[step, side, n], v[s_at, r_at, span, :], preferred_element_type=jnp.float32)
            attend = attend.astype(jnp.bfloat16)
            outs[0, slab, row, here, :] = attend
            delta = jnp.sum(g_rows.astype(jnp.float32) * attend.astype(jnp.float32), axis=1, keepdims=True)
            q_sum = jnp.zeros((TILE, DH), jnp.float32)
            for n in range(3):
                s_at, r_at = group_at(n, slab, row)
                w = weights[step, side, n]
                w_grad = lax.dot_general(
                    g_rows, v[s_at, r_at, span, :], (((1,), (1,)), ((), ())), preferred_element_type=jnp.float32
                )
                s_grad = (w.astype(jnp.float32) * (w_grad - delta) * SCALE).astype(jnp.bfloat16)
                q_sum += jnp.dot(s_grad, k[s_at, r_at, span, :], preferred_element_type=jnp.float32)
                block = n * 6 + slab * 3 + row
                for a, left_side, right_side in ((0, s_grad, q_rows), (1, w, g_rows)):
                    piece = lax.dot_general(
                        left_side, right_side, (((0,), (0,)), ((), ())), preferred_element_type=jnp.float32
                    )
                    if side == 0:
                        group_grads[a, block, 0:REACHED] = piece
                    else:
                        group_grads[a, block, TILE:REACHED] += piece[0 : 2 * TILE]
                        group_grads[a, block, REACHED:SPAN] = piece[2 * TILE :]
            outs[1, slab, row, here, :] = q_sum.astype(jnp.bfloat16)

        @pl.when(step == 3)
        def _():
            gather_groups(0)

        @pl.when(step == 5)
        def _():
            gather_groups(1)
            add_sides(0)
            gather_groups(2)

        @pl.loop(0, 8)
        def _(n):
            at = rem(n + 3 * head, 8)
            send_part(slab, row, div(at, 4), rem(at, 4), outs, (attended, q_grad), send_out.at[0], recv_out.at[0])

    add_sides(1)
    finish(0)
    add_sides(2)
    finish(1)
    finish(2)

    for place in range(3):
        to_right, to_left = side_copies(place)
        to_after, to_before = slab_copies(place)
        for has, copy in ((quarter < 3, to_right), (quarter > 0, to_left), (x < 3, to_after), (x > 0, to_before)):

            @pl.when(has)
            def _():
                copy.wait_send()

    for count in range(4):

        @pl.when(own_parts == count)
        def _():
            for n in range(4):
                wait_bytes(k.at[0, :, 0 : SPAN - 16 * count, :], send_in.at[n])
            for n in range(2):
                wait_bytes(dkv.at[:, 0, :, 0 : SPAN - 16 * count, :], send_out.at[n])

    @pl.when(jnp.logical_not(own_kind))
    def _():
        wait_bytes(flags, kind_sems.at[0])

    wait_bytes(outs, recv_out.at[0])
    wait_bytes(final, recv_out.at[1])


def place_kernel(*refs):
    sources, results, buffers, sems = refs[:4], refs[4:8], refs[8:12], refs[12]
    loads = [pltpu.make_async_copy(s, b, sems.at[n]) for n, (s, b) in enumerate(zip(sources, buffers))]
    stores = [pltpu.make_async_copy(b, r, sems.at[4 + n]) for n, (b, r) in enumerate(zip(buffers, results))]
    for c in loads:
        c.start()
    for load, store in zip(loads, stores):
        load.wait()
        store.start()
    for c in stores:
        c.wait()


def per_device(queries, keys, values, out_grad, key_tiles):
    ctx = lax.axis_index("ctx")
    own_slab = ctx // 2
    lists = key_tiles[0]
    along_time = jnp.any(jnp.logical_and(lists >= 0, lists // 24 != own_slab))
    flags = jnp.broadcast_to(along_time.astype(jnp.int32), (8, 128))

    anywhere = pl.BlockSpec(memory_space=pl.ANY)
    token_block = jax.ShapeDtypeStruct((ROWS, HEADS * DH), jnp.bfloat16)
    near = pltpu.VMEM((4, 3, SPAN, DH), jnp.bfloat16)
    own = pltpu.VMEM((2, 3, COLS, DH), jnp.bfloat16)
    pair = pltpu.VMEM((2, 2, 3, COLS, DH), jnp.bfloat16)
    blocks = pl.pallas_call(
        step_kernel,
        name="attention_step",
        out_shape=(token_block,) * 4,
        in_specs=[anywhere] * 5,
        out_specs=(anywhere,) * 4,
        scratch_shapes=[
            near,
            own,
            near,
            own,
            pltpu.VMEM((6, 2, 3, TILE, REACHED), jnp.bfloat16),
            pltpu.VMEM((2, 19, SPAN, DH), jnp.float32),
            pair,
            pltpu.VMEM((2, 4, 3, SPAN, DH), jnp.bfloat16),
            pltpu.VMEM((2, 2, 4, 3, TILE, DH), jnp.bfloat16),
            pair,
            pltpu.VMEM((2, 4, 3, COLS, DH), jnp.bfloat16),
            pair,
            pltpu.VMEM((8, 128), jnp.int32),
            pltpu.SMEM((8, 128), jnp.int32),
            pltpu.SemaphoreType.DMA((4,)),
            pltpu.SemaphoreType.DMA((4,)),
            pltpu.SemaphoreType.DMA((28,)),
            pltpu.SemaphoreType.DMA((28,)),
            pltpu.SemaphoreType.DMA((3,)),
            pltpu.SemaphoreType.DMA((2,)),
            pltpu.SemaphoreType.DMA((2,)),
            pltpu.SemaphoreType.DMA((2, 3)),
            pltpu.SemaphoreType.DMA((2, 3)),
            pltpu.SemaphoreType.DMA((2, 3)),
            pltpu.SemaphoreType.DMA((2, 3)),
        ],
        compiler_params=pltpu.CompilerParams(has_side_effects=True, collective_id=0, vmem_limit_bytes=VMEM_LIMIT),
    )(keys, queries, values, out_grad, flags)
    return pl.pallas_call(
        place_kernel,
        name="place_results",
        out_shape=(token_block,) * 4,
        in_specs=[anywhere] * 4,
        out_specs=(anywhere,) * 4,
        scratch_shapes=[pltpu.VMEM((ROWS, HEADS * DH), jnp.bfloat16)] * 4 + [pltpu.SemaphoreType.DMA((8,))],
        compiler_params=pltpu.CompilerParams(vmem_limit_bytes=VMEM_LIMIT),
    )(*blocks)


def solution(mesh):
    token_spec = P(("ctx", "head"), None)
    return jax.shard_map(
        per_device,
        mesh=mesh,
        in_specs=(token_spec,) * 4 + (P("head", "ctx", None),),
        out_specs=(token_spec,) * 4,
        check_vma=False,
    )
```

```python
import math

import jax
import jax.numpy as jnp
from jax import lax
from jax.experimental import pallas as pl
from jax.experimental.pallas import tpu as pltpu
from jax.sharding import PartitionSpec as P

DH = 128
TILE = 192
HEADS = 16
PART = 48
ROWS = 144
COLS = 2 * TILE
SPAN = 4 * TILE
REACHED = 3 * TILE
NEG_FILL = -1e30
SCALE = 1.0 / math.sqrt(DH)
LOG2E = 1.0 / math.log(2.0)
MESH = pl.DeviceIdType.MESH
VMEM_LIMIT = 60 * 1024 * 1024


def div(a, b):
    return lax.div(a, jnp.int32(b))


def rem(a, b):
    return lax.rem(a, jnp.int32(b))


def spot():
    ctx, sub = lax.axis_index("ctx"), lax.axis_index("head")
    core, z_hi, x = rem(ctx, 2), rem(div(ctx, 2), 2), div(ctx, 4)
    y, z_lo = rem(sub, 4), div(sub, 4)
    z = z_hi * 4 + z_lo
    head = 2 * z + div(y, 2)
    quarter = 2 * rem(y, 2) + core
    return dict(x=x, y=y, z=z, z_hi=z_hi, sub=sub, core=core, head=head, quarter=quarter)


def worker(x, head, quarter):
    z = div(head, 2)
    y = 2 * rem(head, 2) + div(quarter, 2)
    return (x * 4 + div(z, 4) * 2 + rem(quarter, 2), rem(z, 4) * 4 + y)


def copy_to(src, dst, send, recv, device):
    return pltpu.make_async_remote_copy(
        src_ref=src, dst_ref=dst, send_sem=send, recv_sem=recv, device_id=device, device_id_type=MESH
    )


def greet(me):
    barrier = pltpu.get_barrier_semaphore()
    x = me["x"]
    own = me["sub"] * 4 + me["z_hi"] * 2 + me["core"]

    @pl.loop(1, 64)
    def _(step):
        other = rem(own + step, 64)
        device = (x * 4 + rem(other, 4), div(other, 4))
        pl.semaphore_signal(barrier, inc=1, device_id=device, device_id_type=MESH)

    here = me["z_hi"] * 2 + me["core"]
    for step in (1, 3):
        device = (rem(x + step, 4) * 4 + here, me["sub"])
        pl.semaphore_signal(barrier, inc=1, device_id=device, device_id_type=MESH)
    pl.semaphore_wait(barrier, 65)


def wait_bytes(ref, sem):
    pltpu.make_async_copy(ref, ref, sem).wait()


def step_kernel(
    keys, queries, values, grads, flags,
    attended, q_grad, k_grad, v_grad,
    k, q, v, g, weights, group_grads, outs, dkv, from_side, from_slab, summed, final, kinds, kind,
    send_in, recv_in, halo_send, halo_recv, kind_sems, send_out, recv_out, side_send, side_recv, slab_send, slab_recv
):
    me = spot()
    x, z_hi, core, head, quarter = me["x"], me["z_hi"], me["core"], me["head"], me["quarter"]
    flip = rem(div(head, 2), 2)
    swap = rem(head, 2)

    def row_of(place):
        return place + flip * (2 - 2 * place)

    def part_place(n):
        at = me["sub"] * 3 + n
        tile = core * 12 + div(at, 4)
        column = rem(tile, 8)
        return div(tile, 8), div(column, 2), rem(column, 2), rem(at, 4)

    own_parts = sum((part_place(n)[1] == quarter).astype(jnp.int32) for n in range(3))

    greet(me)

    def send_head(n, target_head, own_head):
        source, out, slab, shift = inputs[n]
        for part_n in range(3):
            row, to, side, part = part_place(part_n)
            first = pl.multiple_of((side + shift) * TILE + part * PART, 16)
            src = source.at[pl.ds(part_n * PART, PART), pl.ds(pl.multiple_of(target_head * DH, DH), DH)]
            dst = out.at[slab, row, pl.ds(first, PART), :]
            remote = copy_to(src, dst, send_in.at[n], recv_in.at[n], worker(x, target_head, to))
            if own_head:

                @pl.when(to == quarter)
                def _():
                    pltpu.make_async_copy(src, dst, recv_in.at[n]).start()

                @pl.when(to != quarter)
                def _():
                    remote.start()

            else:
                remote.start()

    inputs = ((keys, k, 1 + z_hi, 1), (queries, q, z_hi, 0), (values, v, 1 + z_hi, 1), (grads, g, z_hi, 0))

    asker = (
        x * 4 + div(me["sub"], 8) * 2 + core,
        rem(div(me["sub"], 2), 4) * 4 + 2 * rem(me["sub"], 2) + z_hi,
    )
    own_kind = jnp.logical_and(me["sub"] == head, rem(me["y"], 2) == z_hi)

    @pl.when(own_kind)
    def _():
        pltpu.make_async_copy(flags, kinds, kind_sems.at[1]).start()

    @pl.when(jnp.logical_not(own_kind))
    def _():
        copy_to(flags, kinds, kind_sems.at[0], kind_sems.at[1], asker).start()

    for n in range(4):
        pl.loop(1, HEADS)(lambda step: send_head(n, rem(head + step, HEADS), False))
        send_head(n, head, True)

    for a in range(2):
        group_grads[a, 18] = jnp.zeros((SPAN, DH), jnp.float32)

    mine = slice(TILE, TILE + COLS)
    hi, lo = slice(2 * TILE, 3 * TILE), slice(TILE, 2 * TILE)
    top, bottom = slice(3 * TILE, 4 * TILE), slice(0, TILE)
    after = worker(rem(x + 1, 4), head, quarter)
    before = worker(rem(x + 3, 4), head, quarter)

    class Halo:
        def __init__(self, buf, base):
            self.buf, self.base = buf, base
            self.forward = copy_to(
                buf.at[2, :, mine, :], buf.at[0, :, mine, :], halo_send.at[base], halo_recv.at[base], after
            )
            self.backward = copy_to(
                buf.at[1, :, mine, :], buf.at[3, :, mine, :], halo_send.at[base + 1], halo_recv.at[base + 1], before
            )

        def sides(self, n, slabs, action):
            buf, n = self.buf, self.base + n
            to_right, to_left = buf.at[slabs, :, hi, :], buf.at[slabs, :, lo, :]
            at_right, at_left = buf.at[slabs, :, bottom, :], buf.at[slabs, :, top, :]

            def send(j, src, dst, to):
                copy = copy_to(src, dst, halo_send.at[n + j], halo_recv.at[n + j % 2], worker(x, head, to))
                getattr(copy, action)()

            @pl.when(quarter < 3)
            def _():
                send(0, to_right, at_right, rem(quarter + 1, 4))

            @pl.when(quarter > 0)
            def _():
                send(1, to_left, at_left, rem(quarter + 3, 4))

            @pl.when(quarter == 1)
            def _():
                send(2, to_right, at_right, quarter - 1)

            @pl.when(quarter == 2)
            def _():
                send(3, to_left, at_left, quarter + 1)

            if action == "wait_send":
                wait_bytes(at_right, halo_recv.at[n])
                wait_bytes(at_left, halo_recv.at[n + 1])

        def begin(self):
            self.forward.start()
            self.backward.start()
            self.sides(2, slice(1, 3), "start")

        def go_on(self):
            self.forward.wait_recv()
            self.sides(6, 0, "start")
            self.backward.wait_recv()
            self.sides(10, 3, "start")

        def end(self):
            self.sides(2, slice(1, 3), "wait_send")
            self.sides(6, 0, "wait_send")
            self.sides(10, 3, "wait_send")
            self.forward.wait_send()
            self.backward.wait_send()

    key_halo, value_halo = Halo(k, 0), Halo(v, 14)
    wait_bytes(k.at[1:3, :, mine, :], recv_in.at[0])
    key_halo.begin()
    key_halo.go_on()
    wait_bytes(kinds, kind_sems.at[1])
    to_scalar = pltpu.make_async_copy(kinds, kind, kind_sems.at[2])
    to_scalar.start()
    to_scalar.wait()
    along_time = kind[0, 0]
    key_halo.end()
    wait_bytes(q, recv_in.at[1])

    def group_at(n, slab, row):
        return (
            jnp.where(along_time > 0, slab + n, slab + 1),
            jnp.where(along_time > 0, row, jnp.clip(row + n - 1, 0, 2)),
        )

    def places(step):
        return rem(step + swap, 2), row_of(div(step, 2))

    @pl.loop(0, 6)
    def _(step):
        @pl.when(step == 3)
        def _():
            wait_bytes(v.at[1:3, :, mine, :], recv_in.at[2])
            value_halo.begin()

        slab, row = places(step)
        lane = lax.broadcasted_iota(jnp.int32, (1, REACHED), 1)
        for side in range(2):
            rows = q[slab, row, side * TILE : (side + 1) * TILE, :]
            column = 2 * quarter + side
            low = jnp.where(column > 0, 0, TILE)
            high = jnp.where(column < 7, REACHED, 2 * TILE)
            scores = []
            for n in range(3):
                s_at, r_at = group_at(n, slab, row)
                k_rows = k[s_at, r_at, side * TILE : side * TILE + REACHED, :]
                s = lax.dot_general(rows, k_rows, (((1,), (1,)), ((), ())), preferred_element_type=jnp.float32)
                slab_in = 2 * x + slab + n - 1
                ok_time = jnp.logical_and(slab_in >= 0, slab_in < 8).astype(jnp.int32)
                ok_row = jnp.logical_and(row + n - 1 >= 0, row + n - 1 < 3).astype(jnp.int32)
                last = high * jnp.where(along_time > 0, ok_time, ok_row)
                s = s + jnp.where(jnp.logical_and(lane >= low, lane < last), 0.0, NEG_FILL)
                scores.append(s)
            peak = jnp.max(jnp.maximum(jnp.maximum(scores[0], scores[1]), scores[2]), axis=1, keepdims=True)
            raised = [jnp.exp2((s - peak) * (SCALE * LOG2E)) for s in scores]
            share = 1.0 / jnp.sum(raised[0] + raised[1] + raised[2], axis=1, keepdims=True)
            for n in range(3):
                weights[step, side, n] = (raised[n] * share).astype(jnp.bfloat16)

    value_halo.go_on()
    value_halo.end()

    def send_part(slab, row, side, part, arrays, source, targets, send, recv):
        tile = row * 8 + 2 * quarter + side
        at = rem(tile, 12) * 4 + part
        to_core, sub, n = div(tile, 12), div(at, 3), rem(at, 3)
        ctx = x * 4 + slab * 2 + to_core
        self_part = jnp.logical_and(ctx == lax.axis_index("ctx"), sub == me["sub"])
        first = pl.multiple_of(side * TILE + part * PART, 16)
        for a in arrays:
            src = source.at[a, slab, row, pl.ds(first, PART), :]
            dst = targets[a].at[pl.ds(pl.multiple_of(n * PART, 16), PART), pl.ds(pl.multiple_of(head * DH, DH), DH)]

            @pl.when(self_part)
            def _():
                pltpu.make_async_copy(src, dst, recv).start()

            @pl.when(jnp.logical_not(self_part))
            def _():
                copy_to(src, dst, send, recv, (ctx, sub)).start()

    def send_out_part(slab, row, at, a):
        send_part(slab, row, div(at, 4), rem(at, 4), (a,), outs, (attended, q_grad), send_out.at[0], recv_out.at[0])

    @pl.loop(0, 6)
    def _(step):
        slab, row = places(step)
        for side in range(2):
            span = slice(side * TILE, side * TILE + REACHED)
            attend = jnp.zeros((TILE, DH), jnp.float32)
            for n in range(3):
                s_at, r_at = group_at(n, slab, row)
                attend += jnp.dot(weights[step, side, n], v[s_at, r_at, span, :], preferred_element_type=jnp.float32)
            outs[0, slab, row, side * TILE : (side + 1) * TILE, :] = attend.astype(jnp.bfloat16)

        @pl.loop(0, 8)
        def _(n):
            send_out_part(slab, row, rem(n + 3 * head, 8), 0)

    wait_bytes(g, recv_in.at[3])

    def side_copies(place):
        row = row_of(place)
        left = worker(x, head, rem(quarter + 3, 4))
        right = worker(x, head, rem(quarter + 1, 4))
        return (
            copy_to(
                dkv.at[:, :, row, top, :], from_side.at[0, :, :, row], side_send.at[0, place], side_recv.at[0, place], right
            ),
            copy_to(
                dkv.at[:, :, row, bottom, :], from_side.at[1, :, :, row], side_send.at[1, place], side_recv.at[1, place], left
            ),
        )

    def gather_groups(place):
        row = row_of(place)
        for s_at in range(4):
            if 1 <= s_at <= 2:
                same = 6 + (s_at - 1) * 3 + row
                previous = jnp.where(
                    along_time > 0,
                    s_at * 3 + row if s_at < 2 else 18,
                    jnp.where(row < 2, (s_at - 1) * 3 + row + 1, 18),
                )
                following = jnp.where(
                    along_time > 0,
                    12 + (s_at - 2) * 3 + row if s_at >= 2 else 18,
                    jnp.where(row > 0, 12 + (s_at - 1) * 3 + row - 1, 18),
                )
                for a in range(2):
                    total = group_grads[a, same] + group_grads[a, previous] + group_grads[a, following]
                    dkv[a, s_at, row] = total.astype(jnp.bfloat16)
            else:
                only = jnp.where(along_time > 0, row if s_at == 0 else 15 + row, 18)
                for a in range(2):
                    dkv[a, s_at, row] = group_grads[a, only].astype(jnp.bfloat16)
        to_right, to_left = side_copies(place)

        @pl.when(quarter < 3)
        def _():
            to_right.start()

        @pl.when(quarter > 0)
        def _():
            to_left.start()

    @pl.loop(0, 6)
    def _(step):
        slab, row = places(step)
        for side in range(2):
            here = slice(side * TILE, (side + 1) * TILE)
            span = slice(side * TILE, side * TILE + REACHED)
            q_rows, g_rows = q[slab, row, here, :], g[slab, row, here, :]
            attend = outs[0, slab, row, here, :]
            delta = jnp.sum(g_rows.astype(jnp.float32) * attend.astype(jnp.float32), axis=1, keepdims=True)
            q_sum = jnp.zeros((TILE, DH), jnp.float32)
            for n in range(3):
                s_at, r_at = group_at(n, slab, row)
                w = weights[step, side, n]
                w_grad = lax.dot_general(
                    g_rows, v[s_at, r_at, span, :], (((1,), (1,)), ((), ())), preferred_element_type=jnp.float32
                )
                s_grad = (w.astype(jnp.float32) * (w_grad - delta) * SCALE).astype(jnp.bfloat16)
                q_sum += jnp.dot(s_grad, k[s_at, r_at, span, :], preferred_element_type=jnp.float32)
                block = n * 6 + slab * 3 + row
                for a, left_side, right_side in ((0, s_grad, q_rows), (1, w, g_rows)):
                    piece = lax.dot_general(
                        left_side, right_side, (((0,), (0,)), ((), ())), preferred_element_type=jnp.float32
                    )
                    if side == 0:
                        group_grads[a, block, 0:REACHED] = piece
                    else:
                        group_grads[a, block, TILE:REACHED] += piece[0 : 2 * TILE]
                        group_grads[a, block, REACHED:SPAN] = piece[2 * TILE :]
            outs[1, slab, row, here, :] = q_sum.astype(jnp.bfloat16)

        @pl.loop(0, 8)
        def _(n):
            at = rem(n + 3 * head, 8)
            send_out_part(slab, row, at, 1)

        @pl.when(step == 3)
        def _():
            gather_groups(0)

    gather_groups(1)
    gather_groups(2)

    def slab_copies(place):
        row = row_of(place)
        return (
            copy_to(summed.at[:, 3, row], from_slab.at[0, :, row], slab_send.at[0, place], slab_recv.at[0, place], after),
            copy_to(summed.at[:, 0, row], from_slab.at[1, :, row], slab_send.at[1, place], slab_recv.at[1, place], before),
        )

    for place in range(3):
        row = row_of(place)
        for side in range(2):
            has = quarter > 0 if side == 0 else quarter < 3
            here = slice((1 + side) * TILE, (2 + side) * TILE)
            there = slice(side * TILE, (1 + side) * TILE)

            @pl.when(has)
            def _():
                wait_bytes(from_side.at[side, :, :, row], side_recv.at[side, place])
                for a in range(2):
                    for s in range(4):
                        summed[a, s, row, there, :] = (
                            dkv[a, s, row, here, :].astype(jnp.float32) + from_side[side, a, s, row].astype(jnp.float32)
                        ).astype(jnp.bfloat16)

            @pl.when(jnp.logical_not(has))
            def _():
                for a in range(2):
                    for s in range(4):
                        summed[a, s, row, there, :] = dkv[a, s, row, here, :]

        to_after, to_before = slab_copies(place)

        @pl.when(x < 3)
        def _():
            to_after.start()

        @pl.when(x > 0)
        def _():
            to_before.start()

    for place in range(3):
        row = row_of(place)
        for slab in range(2):
            has = x > 0 if slab == 0 else x < 3

            @pl.when(has)
            def _():
                wait_bytes(from_slab.at[slab, :, row], slab_recv.at[slab, place])
                for a in range(2):
                    final[a, slab, row] = (
                        summed[a, 1 + slab, row].astype(jnp.float32) + from_slab[slab, a, row].astype(jnp.float32)
                    ).astype(jnp.bfloat16)

            @pl.when(jnp.logical_not(has))
            def _():
                for a in range(2):
                    final[a, slab, row] = summed[a, 1 + slab, row]

        @pl.loop(0, 16)
        def _(n):
            at = rem(n + 3 * head, 16)
            send_part(
                div(at, 8), row, rem(div(at, 4), 2), rem(at, 4), (0, 1), final, (k_grad, v_grad), send_out.at[1], recv_out.at[1]
            )

    for place in range(3):
        to_right, to_left = side_copies(place)
        to_after, to_before = slab_copies(place)
        for has, copy in ((quarter < 3, to_right), (quarter > 0, to_left), (x < 3, to_after), (x > 0, to_before)):

            @pl.when(has)
            def _():
                copy.wait_send()

    for count in range(4):

        @pl.when(own_parts == count)
        def _():
            for n in range(4):
                wait_bytes(k.at[0, :, 0 : SPAN - 16 * count, :], send_in.at[n])
            for n in range(2):
                wait_bytes(dkv.at[:, 0, :, 0 : SPAN - 16 * count, :], send_out.at[n])

    @pl.when(jnp.logical_not(own_kind))
    def _():
        wait_bytes(flags, kind_sems.at[0])

    wait_bytes(outs, recv_out.at[0])
    wait_bytes(final, recv_out.at[1])


def place_kernel(*refs):
    sources, results, buffers, sems = refs[:4], refs[4:8], refs[8:12], refs[12]
    loads = [pltpu.make_async_copy(s, b, sems.at[n]) for n, (s, b) in enumerate(zip(sources, buffers))]
    stores = [pltpu.make_async_copy(b, r, sems.at[4 + n]) for n, (b, r) in enumerate(zip(buffers, results))]
    for c in loads:
        c.start()
    for load, store in zip(loads, stores):
        load.wait()
        store.start()
    for c in stores:
        c.wait()


def per_device(queries, keys, values, out_grad, key_tiles):
    ctx = lax.axis_index("ctx")
    own_slab = ctx // 2
    lists = key_tiles[0]
    along_time = jnp.any(jnp.logical_and(lists >= 0, lists // 24 != own_slab))
    flags = jnp.broadcast_to(along_time.astype(jnp.int32), (8, 128))

    anywhere = pl.BlockSpec(memory_space=pl.ANY)
    token_block = jax.ShapeDtypeStruct((ROWS, HEADS * DH), jnp.bfloat16)
    near = pltpu.VMEM((4, 3, SPAN, DH), jnp.bfloat16)
    own = pltpu.VMEM((2, 3, COLS, DH), jnp.bfloat16)
    pair = pltpu.VMEM((2, 2, 3, COLS, DH), jnp.bfloat16)
    blocks = pl.pallas_call(
        step_kernel,
        name="attention_step",
        out_shape=(token_block,) * 4,
        in_specs=[anywhere] * 5,
        out_specs=(anywhere,) * 4,
        scratch_shapes=[
            near,
            own,
            near,
            own,
            pltpu.VMEM((6, 2, 3, TILE, REACHED), jnp.bfloat16),
            pltpu.VMEM((2, 19, SPAN, DH), jnp.float32),
            pair,
            pltpu.VMEM((2, 4, 3, SPAN, DH), jnp.bfloat16),
            pltpu.VMEM((2, 2, 4, 3, TILE, DH), jnp.bfloat16),
            pair,
            pltpu.VMEM((2, 4, 3, COLS, DH), jnp.bfloat16),
            pair,
            pltpu.VMEM((8, 128), jnp.int32),
            pltpu.SMEM((8, 128), jnp.int32),
            pltpu.SemaphoreType.DMA((4,)),
            pltpu.SemaphoreType.DMA((4,)),
            pltpu.SemaphoreType.DMA((28,)),
            pltpu.SemaphoreType.DMA((28,)),
            pltpu.SemaphoreType.DMA((3,)),
            pltpu.SemaphoreType.DMA((2,)),
            pltpu.SemaphoreType.DMA((2,)),
            pltpu.SemaphoreType.DMA((2, 3)),
            pltpu.SemaphoreType.DMA((2, 3)),
            pltpu.SemaphoreType.DMA((2, 3)),
            pltpu.SemaphoreType.DMA((2, 3)),
        ],
        compiler_params=pltpu.CompilerParams(has_side_effects=True, collective_id=0, vmem_limit_bytes=VMEM_LIMIT),
    )(keys, queries, values, out_grad, flags)
    return pl.pallas_call(
        place_kernel,
        name="place_results",
        out_shape=(token_block,) * 4,
        in_specs=[anywhere] * 4,
        out_specs=(anywhere,) * 4,
        scratch_shapes=[pltpu.VMEM((ROWS, HEADS * DH), jnp.bfloat16)] * 4 + [pltpu.SemaphoreType.DMA((8,))],
        compiler_params=pltpu.CompilerParams(vmem_limit_bytes=VMEM_LIMIT),
    )(*blocks)


def solution(mesh):
    token_spec = P(("ctx", "head"), None)
    return jax.shard_map(
        per_device,
        mesh=mesh,
        in_specs=(token_spec,) * 4 + (P("head", "ctx", None),),
        out_specs=(token_spec,) * 4,
        check_vma=False,
    )
```
